128 devices in a mesh: row: 8 (over x, core), col: 16 (over y, z).
Axes of the slice: x: 4, y: 4, z: 4, core: 2. Of those that a mesh axis runs over, the one named last changes fastest.
Arguments:
- local_load: float32 [8, 16, 1024, 256], P('row', 'col'), may hold values from -6 to 6
- schur_operator: float32 [8, 16, 1024, 1024], P('row', 'col'), may hold values from -1 to 5
- local_solver: float32 [8, 16, 1024, 1024], P('row', 'col'), may hold values from -1 to 1
- coarse_modes: float32 [8, 16, 32, 1024], P('row', 'col'), may hold values from -0.1875 to 0.1875
- coarse_inverse: float32 [8, 16, 8, 32, 512], P('row', 'col'), may hold values from -1 to 2
- share_rows: int32 [8, 16, 3, 3, 128], P('row', 'col'), may hold values from 0 to 1023, as said below
- share_count: int32 [8, 16, 3, 3], P('row', 'col'), may hold values from 0 to 128, as said below
- multiplicity: int32 [8, 16, 1024], P('row', 'col'), may hold values from 1 to 2, as said below
Outputs:
- iterate: float32 [8, 16, 1024, 256], P('row', 'col')
- residual: float32 [8, 16, 1024, 256], P('row', 'col')
The draws below stay inside these ranges and needn't reach their ends.
Inputs may be any that keep to these rules, and one draw needn't show every extreme that they name: `share_rows`: within one subdomain no row lies in two lists, and only the first share_count entries of a list are meaningful. Entry m of the list of (a, b) toward (a + p - 1, b + q - 1) and entry m of that neighbour's list toward (a, b) name the same interface unknown. share_count[a, b, p, q] equals the neighbour's count toward (a, b); it is 0 for the centre and where no neighbour exists, at most 128 along a grid axis and at most 16 for a diagonal neighbour, and both bounds are reached. multiplicity is 2 on rows that lie in some list and 1 elsewhere.
All inputs are finite; a program needn't handle non-finite values.
Results may differ from the reference program's by a relative error of at most 0.0003.
Values sent between devices are 32-bit elements; how exact they have to be, the bound alone decides.
No kernel may reach another device: no remote copies, remote signals or barrier semaphores. Data moves between devices by JAX's collectives and lax.ppermute only.
A program may use at most 128 MiB of HBM per device.

```python
import math
import jax
import jax.numpy as jnp
import numpy as np
from jax import lax

NI = 1024
R = 256
MODES = 32
SHARE = 128
CORNER = 16
STEPS = 2
GRID_ROWS = 8
GRID_COLS = 16


def shifted_drawn(array_in, row_by, col_by):
    row_count, col_count = (array_in.shape[0], array_in.shape[1])
    padded = jnp.pad(array_in, ((1, 1), (1, 1)) + ((0, 0),) * (array_in.ndim - 2))
    return padded[1 - row_by:1 - row_by + row_count, 1 - col_by:1 - col_by + col_count]


def slot_layout():
    starts = np.array([[4 * SHARE, 0, 4 * SHARE + CORNER], [SHARE, 0, 2 * SHARE], [4 * SHARE + 2 * CORNER, 3 * SHARE, 4 * SHARE + 3 * CORNER]], np.int32)
    slot_sizes = np.array([[CORNER, SHARE, CORNER], [SHARE, 0, SHARE], [CORNER, SHARE, CORNER]], np.int32)
    return (starts, slot_sizes)


def sharing(key):
    base_key = jax.random.fold_in(key, 7)
    perm_key, face_key, corner_key, filler_key = jax.random.split(base_key, 4)
    perm_keys = jax.random.split(perm_key, GRID_ROWS * GRID_COLS)
    permutations = jax.vmap(lambda sub_key: jax.random.permutation(sub_key, NI))(perm_keys)
    permutations = permutations.reshape(GRID_ROWS, GRID_COLS, NI).astype(jnp.int32)
    face_counts = jax.random.randint(face_key, (GRID_ROWS, GRID_COLS, 2), SHARE // 2, SHARE + 1).astype(jnp.int32)
    corner_counts = jax.random.randint(corner_key, (GRID_ROWS, GRID_COLS, 2), 1, CORNER + 1).astype(jnp.int32)
    face_counts = face_counts.at[0, 0, 0].set(SHARE)
    corner_counts = corner_counts.at[0, 0, 0].set(CORNER)
    row_ids = jnp.arange(GRID_ROWS)[:, None]
    col_ids = jnp.arange(GRID_COLS)[None, :]
    east_counts = jnp.where(col_ids < GRID_COLS - 1, face_counts[:, :, 0], 0)
    south_counts = jnp.where(row_ids < GRID_ROWS - 1, face_counts[:, :, 1], 0)
    south_east = jnp.where((row_ids < GRID_ROWS - 1) & (col_ids < GRID_COLS - 1), corner_counts[:, :, 0], 0)
    south_west = jnp.where((row_ids < GRID_ROWS - 1) & (col_ids > 0), corner_counts[:, :, 1], 0)
    no_counts = jnp.zeros_like(east_counts)
    count_table = [[shifted_drawn(south_east, 1, 1), shifted_drawn(south_counts, 1, 0), shifted_drawn(south_west, 1, -1)], [shifted_drawn(east_counts, 0, 1), no_counts, east_counts], [south_west, south_counts, south_east]]
    counts = jnp.stack([jnp.stack(count_line, axis=-1) for count_line in count_table], axis=-2).astype(jnp.int32)
    starts, slot_sizes = slot_layout()
    slot_ids = np.arange(SHARE, dtype=np.int32)
    positions = starts[:, :, None] + np.minimum(slot_ids[None, None, :], np.maximum(slot_sizes - 1, 0)[:, :, None])
    listed = permutations[:, :, positions]
    filler = jax.random.randint(filler_key, listed.shape, 0, NI).astype(jnp.int32)
    share_rows = jnp.where(jnp.asarray(slot_ids) < counts[..., None], listed, filler).astype(jnp.int32)
    slot_iota = jnp.arange(NI, dtype=jnp.int32)
    shared_flag = jnp.zeros((GRID_ROWS, GRID_COLS, NI), jnp.int32)
    for row_slot in range(3):
        for col_slot in range(3):
            first_slot = int(starts[row_slot, col_slot])
            used_count = counts[:, :, row_slot, col_slot][:, :, None]
            inside = (slot_iota >= first_slot) & (slot_iota < first_slot + used_count)
            shared_flag = shared_flag + inside.astype(jnp.int32)
    inverse_perm = jnp.argsort(permutations, axis=-1).astype(jnp.int32)
    multiplicity = jnp.take_along_axis(1 + shared_flag, inverse_perm, axis=-1).astype(jnp.int32)
    return (share_rows, counts, multiplicity)


def draw_share_rows(key, part):
    return sharing(key)[0]


def draw_share_count(key, part):
    return sharing(key)[1]


def draw_multiplicity(key, part):
    return sharing(key)[2]


def operator_noise(noise_key):
    full_shape = (GRID_ROWS, GRID_COLS, NI, NI)
    return jnp.clip(jax.random.normal(noise_key, full_shape, jnp.float32), -5.0, 5.0)


def diagonal_values(key):
    base_key = jax.random.fold_in(key, 19)
    return jax.random.uniform(base_key, (GRID_ROWS, GRID_COLS, NI), jnp.float32, 2.0, 4.0)


def draw_schur_operator(key, part):
    diagonal = diagonal_values(key)
    noise_key = jax.random.fold_in(jax.random.fold_in(key, 29), 0)
    identity = jnp.eye(NI, dtype=jnp.float32)
    return identity * diagonal[..., None] + 0.5 / math.sqrt(NI) * operator_noise(noise_key)


def draw_local_solver(key, part):
    diagonal = diagonal_values(key)
    noise_key = jax.random.fold_in(jax.random.fold_in(key, 31), 0)
    identity = jnp.eye(NI, dtype=jnp.float32)
    return identity * (1.0 / diagonal)[..., None] + 0.1 / math.sqrt(NI) * operator_noise(noise_key)


def draw_coarse_inverse(key, part):
    base_key = jax.random.fold_in(key, 23)
    noise_key, diag_key = jax.random.split(base_key)
    tile_width = GRID_COLS * MODES
    full_shape = (GRID_ROWS, GRID_COLS, GRID_ROWS, MODES, tile_width)
    noise_scale = 0.5 / math.sqrt(MODES * GRID_ROWS * GRID_COLS)
    noise_one = jnp.clip(jax.random.normal(noise_key, full_shape, jnp.float32), -5.0, 5.0)
    same_row = lax_iota(full_shape, 0) == lax_iota(full_shape, 2)
    same_col = lax_iota(full_shape, 4) == lax_iota(full_shape, 1) * MODES + lax_iota(full_shape, 3)
    diagonal = jax.random.uniform(diag_key, full_shape, jnp.float32, 0.5, 1.0)
    return noise_one * noise_scale + jnp.where(same_row & same_col, diagonal, 0.0)


def lax_iota(full_shape, dimension):
    return jax.lax.broadcasted_iota(jnp.int32, full_shape, dimension)


def level_of(stream_key, extent, shards, smallest, high):
    def one(dim, parts):
        steps = jax.random.uniform(jax.random.fold_in(jax.random.fold_in(stream_key, 6), dim), (parts,), jnp.float32, smallest / len(shards), high / len(shards))
        return jnp.repeat(jnp.exp(steps), extent[dim] // parts).reshape((-1,) + (1,) * (len(extent) - dim - 1))

    level = one(*shards[0])
    for cut in shards[1:]:
        level = level * one(*cut)
    return level


def gaussian(stream_key, shape, scale, reach, shards=(), held_as=jnp.bfloat16):
    result = jax.random.normal(stream_key, shape, jnp.float32) * scale
    if len(shards) > 0:
        result = level_of(stream_key, shape, shards, -0.22, 0.18) * result
    return jnp.clip(result, min=-reach, max=reach).astype(held_as)


def setup_inputs(seed: int = 0) -> dict:
    key_of = jax.random.split(jax.random.key(seed), 9)
    return {
        "local_load": gaussian(key_of[0], (GRID_ROWS, GRID_COLS, NI, R), 1.0, 6.0, ((0, 8), (1, 16)), jnp.float32),
        "schur_operator": draw_schur_operator(jax.random.fold_in(key_of[8], 71), 0),
        "local_solver": draw_local_solver(jax.random.fold_in(key_of[8], 71), 0),
        "coarse_modes": gaussian(key_of[3], (GRID_ROWS, GRID_COLS, MODES, NI), NI ** -0.5, 0.1875, ((0, 8), (1, 16)), jnp.float32),
        "coarse_inverse": draw_coarse_inverse(jax.random.fold_in(key_of[8], 71), 0),
        "share_rows": draw_share_rows(jax.random.fold_in(key_of[8], 71), 0),
        "share_count": draw_share_count(jax.random.fold_in(key_of[8], 71), 0),
        "multiplicity": draw_multiplicity(jax.random.fold_in(key_of[8], 71), 0),
    }


PRECISE = lax.Precision.HIGHEST


def shifted(array_in, row_by, col_by):
    row_count, col_count = array_in.shape[0], array_in.shape[1]
    padded = jnp.pad(array_in, ((1, 1), (1, 1)) + ((0, 0),) * (array_in.ndim - 2))
    return padded[1 - row_by:1 - row_by + row_count, 1 - col_by:1 - col_by + col_count]


def pick_rows(values, indices):
    return values[indices]


def add_rows(values, indices, arrived):
    return values.at[indices.reshape(-1)].add(arrived.reshape(-1, arrived.shape[-1]))


def assemble(values, share_rows, share_count):
    slot_ids = jnp.arange(share_rows.shape[-1], dtype=jnp.int32)
    live_mask = (slot_ids < share_count[..., None]).astype(values.dtype)
    packets = jax.vmap(jax.vmap(pick_rows))(values, share_rows) * live_mask[..., None]
    count_lines = []
    for row_slot in range(3):
        count_line = []
        for col_slot in range(3):
            count_line.append(shifted(packets[:, :, 2 - row_slot, 2 - col_slot], 1 - row_slot, 1 - col_slot))
        count_lines.append(jnp.stack(count_line, axis=2))
    incoming = jnp.stack(count_lines, axis=2)
    return jax.vmap(jax.vmap(add_rows))(values, share_rows, incoming)


def apply_matrix(matrix, vector):
    return jnp.einsum('abij,abjr->abir', matrix, vector, precision=PRECISE)


def reference(local_load, schur_operator, local_solver, coarse_modes, coarse_inverse, share_rows, share_count, multiplicity):
    weight = (1.0 / multiplicity.astype(jnp.float32))[..., None]
    residual = assemble(local_load, share_rows, share_count)
    iterate = jnp.zeros_like(residual)
    for step_index in range(STEPS):
        coarse_rhs = jnp.einsum('abmi,abir->abmr', coarse_modes, weight * residual, precision=PRECISE)
        coarse_sol = jnp.einsum('abcmk,cbmr->akr', coarse_inverse, coarse_rhs, precision=PRECISE)
        coarse_sol = coarse_sol.reshape(GRID_ROWS, GRID_COLS, MODES, coarse_sol.shape[-1])
        spread_values = weight * jnp.einsum('abmi,abmr->abir', coarse_modes, coarse_sol, precision=PRECISE)
        correction = assemble(spread_values, share_rows, share_count)
        iterate = iterate + correction
        residual = residual - assemble(apply_matrix(schur_operator, correction), share_rows, share_count)
        update = assemble(weight * apply_matrix(local_solver, weight * residual), share_rows, share_count)
        iterate = iterate + update
        residual = residual - assemble(apply_matrix(schur_operator, update), share_rows, share_count)
    return iterate, residual
```

```python
import functools

import jax
import jax.numpy as jnp
from jax import lax
from jax.experimental import pallas as pl
from jax.experimental.pallas import tpu as pltpu
from jax.sharding import PartitionSpec as P

NI = 1024
RHS = 256
MODES = 32
FACE = 128
CORNER = 16
STEPS = 2
BUNDLE = FACE + 2 * CORNER
SLOTS = 2 * BUNDLE + 2 * FACE
NB = 640
NX = NI - NB
F32 = jnp.float32
BF16 = jnp.bfloat16


def dot(a, b):
    return jnp.dot(a, b, preferred_element_type=F32)


def dot_t(a, b):
    return lax.dot_general(a, b, (((0,), (0,)), ((), ())), preferred_element_type=F32)


def split(v):
    high = v.astype(BF16)
    return high, (v - high.astype(F32)).astype(BF16)


def product(mat_high, mat_low, v, mul=dot):
    high, low = split(v)
    return mul(mat_high, high) + mul(mat_high, low) + mul(mat_low, high)


def select(onehot, v):
    high, low = split(v)
    return dot(onehot, high) + dot(onehot, low)


def call(body, out_shapes, args, scratch=(), smem=0, limit=32):
    specs = [pl.BlockSpec(memory_space=pltpu.SMEM)] * smem
    specs += [pl.BlockSpec(memory_space=pltpu.VMEM)] * (len(args) - smem)
    return pl.pallas_call(
        body,
        out_shape=[jax.ShapeDtypeStruct(s, d) for s, d in out_shapes],
        in_specs=specs,
        out_specs=[pl.BlockSpec(memory_space=pltpu.VMEM)] * len(out_shapes),
        scratch_shapes=list(scratch),
        compiler_params=pltpu.CompilerParams(vmem_limit_bytes=limit << 20),
    )(*args)


VEC_B = ((NB, RHS), F32)
VEC_X = ((NX, RHS), F32)
PACKETS = [((BUNDLE, RHS), F32)] * 2 + [((FACE, RHS), F32)] * 2


def put_packets(v, refs):
    east, west, north, south = refs
    east[...] = v[:BUNDLE]
    west[...] = v[BUNDLE : 2 * BUNDLE]
    north[...] = v[2 * BUNDLE : 2 * BUNDLE + FACE]
    south[...] = v[2 * BUNDLE + FACE : SLOTS]


def received(arrivals, mask_ref):
    from_east, from_west, from_north, from_south = (ref[...] for ref in arrivals)
    end = CORNER + FACE
    whole = jnp.concatenate(
        [
            from_north[end:],
            from_east[CORNER:end],
            from_south[end:],
            from_north[:CORNER],
            from_west[CORNER:end],
            from_south[:CORNER],
            from_north[CORNER:end],
            from_south[CORNER:end],
            jnp.zeros((NB - SLOTS, RHS), F32),
        ],
        axis=0,
    )
    mask = mask_ref[...]
    return whole * jnp.concatenate([mask, mask], axis=1)


def order_body(slots_ref, mult_ref, load_ref, to_slots, to_rows, mask_ref, weight_ref, vb, vx, e, w, n, s, upper):
    slots = slots_ref[...]
    live = slots >= 0
    inner = mult_ref[...] == 1
    lane = lax.broadcasted_iota(jnp.int32, (1, NI), 1)
    row16 = lax.broadcasted_iota(jnp.int32, (16, NI), 0)
    free_f = jnp.where(live, 0.0, 1.0)
    inner_f = jnp.where(inner, 1.0, 0.0)
    stacked = jnp.where(row16 == 0, free_f, jnp.where(row16 == 1, inner_f, 0.0)).astype(BF16)
    for blk in range(8):
        rows = lax.broadcasted_iota(jnp.int32, (128, NI), 0) + 128 * blk
        cols = lax.broadcasted_iota(jnp.int32, (128, NI), 1)
        upper[128 * blk : 128 * (blk + 1), :] = jnp.where(rows < cols, 1.0, 0.0).astype(BF16)
    ranks = dot(stacked, upper[...])
    slot_key = jnp.where(live, slots.astype(F32), NI + ranks[0:1])
    row_key = jnp.where(inner, NI + ranks[1:2], lane.astype(F32))
    live_f = 1.0 - free_f
    row128 = lax.broadcasted_iota(jnp.int32, (128, NI), 0)
    keys = jnp.where(row128 == 0, slot_key, jnp.where(row128 == 1, row_key, live_f))
    columns = jnp.transpose(keys)
    for blk in range(8):
        part = columns[128 * blk : 128 * (blk + 1)]
        to_slots[128 * blk : 128 * (blk + 1), :] = jnp.where(part[:, 0:1] == row_key, 1.0, 0.0).astype(BF16)
        to_rows[128 * blk : 128 * (blk + 1), :] = jnp.where(part[:, 1:2] == slot_key, 1.0, 0.0).astype(BF16)
    mask_ref[...] = jnp.broadcast_to(columns[:NB, 2:3], (NB, 128))
    weight_ref[...] = 1.0 - 0.5 * live_f
    v = select(to_slots[...], load_ref[...])
    vb[...] = v[:NB]
    vx[...] = v[NB:]
    put_packets(v, (e, w, n, s))


def reorder_body(first, count, scaled, mat_ref, to_slots, to_rows, weight_ref, out_ref, high, low):
    for blk in range(4):
        rows = slice(256 * blk, 256 * (blk + 1))
        a, b = split(mat_ref[rows, :])
        high[rows, :] = a
        low[rows, :] = b
    size = 128

    def step(i, carry):
        pick = to_slots[pl.ds(pl.multiple_of(first + i * size, size), size), :]
        where = pl.ds(pl.multiple_of(i * size, size), size)
        if scaled:
            sub = lax.broadcasted_iota(jnp.int32, (size, NI), 0) + (first + i * size)
            lanes = lax.broadcasted_iota(jnp.int32, (size, NI), 1)
            own = jnp.sum(jnp.where(sub == lanes, weight_ref[...], 0.0), axis=1, keepdims=True)
            scale = own * weight_ref[...]
        for level, src in enumerate((high, low)):
            moved = dot(pick, src[...]).astype(BF16)
            placed = dot(moved, to_rows[...])
            if scaled:
                placed = placed * scale
            out_ref[level, where, :] = placed.astype(BF16)
        return carry

    lax.fori_loop(0, count // size, step, 0)


def small_body(modes_ref, tile_ref, to_rows, weight_ref, modes_out, tile_out):
    high, low = split(modes_ref[...])
    modes_out[0] = (dot(high, to_rows[...]) * weight_ref[...]).astype(BF16)
    modes_out[1] = (dot(low, to_rows[...]) * weight_ref[...]).astype(BF16)
    a, b = split(jnp.transpose(tile_ref[...]))
    tile_out[0] = a
    tile_out[1] = b


def first_body(vb, vx, fe, fw, fn, fs, mask, modes, rb_out, rhs_out):
    rb = vb[...] + received((fe, fw, fn, fs), mask)
    rb_out[...] = rb
    rhs_out[...] = product(modes[0, :, :NB], modes[1, :, :NB], rb) + product(modes[0, :, NB:], modes[1, :, NB:], vx[...])


def coarse_body(place, own, one, three, two, partner, tile, keep, out_one, out_three, out_two, gathered):
    chip, core, group = place[0], place[1], place[2]
    for side in range(2):
        which = core if side == 0 else 1 - core
        for slot, (ref, shift) in enumerate(((own, 0), (one, 1), (three, 3), (two, 2))):
            block = 2 * lax.rem(chip + 4 - shift, 4) + which
            value = ref[...] if side == 0 else partner[slot * MODES : (slot + 1) * MODES]
            gathered[pl.ds(pl.multiple_of(block * MODES, MODES), MODES), :] = value
    high, low = split(gathered[...])
    for ref, shift in ((out_one, 1), (out_three, 3), (out_two, 2), (keep, 0)):
        rows = pl.ds(pl.multiple_of(lax.rem(group + shift, 4) * FACE, FACE), FACE)
        mat_high, mat_low = tile[0, rows, :], tile[1, rows, :]
        ref[...] = dot(mat_high, high) + dot(mat_high, low) + dot(mat_low, high)


def middle_body(place, keep, one, three, two, own, out_one, out_three, out_two, total):
    member = place[3]
    total[...] = (keep[...] + one[...]) + (three[...] + two[...])
    for ref, shift in ((own, 0), (out_one, 1), (out_three, 3), (out_two, 2)):
        rows = pl.ds(pl.multiple_of(lax.rem(member + shift, 4) * MODES, MODES), MODES)
        ref[...] = total[rows, :]


def spread_body(own, one, three, two, modes, sol_out, cb, e, w, n, s):
    sol = (own[...] + one[...]) + (three[...] + two[...])
    sol_out[...] = sol
    v = product(modes[0, :, :NB], modes[1, :, :NB], sol, dot_t)
    cb[...] = v
    put_packets(v, (e, w, n, s))


def spread_rest_body(sol, modes, mat, cx_out, pre_out):
    cx = product(modes[0, :, NB:], modes[1, :, NB:], sol[...], dot_t)
    cx_out[...] = cx
    pre_out[...] = product(mat[0, :, NB:], mat[1, :, NB:], cx)


def apply_body(pb, fe, fw, fn, fs, mask, pre, mat, vb_out, tb, e, w, n, s):
    vb = pb[...] + received((fe, fw, fn, fs), mask)
    vb_out[...] = vb
    t = pre[...] + product(mat[0, :, :NB], mat[1, :, :NB], vb)
    tb[...] = t
    put_packets(t, (e, w, n, s))


def solve_body(rb, pb, fe, fw, fn, fs, mask, pre, mat, rb_out, tb, e, w, n, s):
    r = rb[...] - (pb[...] + received((fe, fw, fn, fs), mask))
    rb_out[...] = r
    t = pre[...] + product(mat[0, :, :NB], mat[1, :, :NB], r)
    tb[...] = t
    put_packets(t, (e, w, n, s))


def apply_rest_body(fresh, vb, vx, rx, xb, xx, mat, nxt, rx_out, pre_out, xb_out, xx_out):
    b, x = vb[...], vx[...]
    t = product(mat[0, :, :NB], mat[1, :, :NB], b) + product(mat[0, :, NB:], mat[1, :, NB:], x)
    r = rx[...] - t
    rx_out[...] = r
    if nxt is not None:
        pre_out[...] = product(nxt[0, :, NB:], nxt[1, :, NB:], r)
    xb_out[...] = b if fresh else xb[...] + b
    xx_out[...] = x if fresh else xx[...] + x


def solve_rest_body(rb, rx, mat, nxt, gx_out, pre_out):
    g = product(mat[0, :, :NB], mat[1, :, :NB], rb[...]) + product(mat[0, :, NB:], mat[1, :, NB:], rx[...])
    gx_out[...] = g
    pre_out[...] = product(nxt[0, :, NB:], nxt[1, :, NB:], g)


def close_body(rb, tb, fe, fw, fn, fs, mask, modes, pre, rb_out, rhs_out):
    r = rb[...] - (tb[...] + received((fe, fw, fn, fs), mask))
    rb_out[...] = r
    rhs_out[...] = pre[...] + product(modes[0, :, :NB], modes[1, :, :NB], r)


def final_pre_body(xb, xx, rx, to_rows, it_out, pre_out):
    it_out[...] = select(to_rows[:, :NB], xb[...]) + select(to_rows[:, NB:], xx[...])
    pre_out[...] = select(to_rows[:, NB:], rx[...])


def final_body(rb, tb, fe, fw, fn, fs, mask, to_rows, pre, res_out):
    r = rb[...] - (tb[...] + received((fe, fw, fn, fs), mask))
    res_out[...] = pre[...] + select(to_rows[:, :NB], r)


def on_device(rows, cols, local_load, schur, solver, modes, inverse, share_rows, share_count, mult):
    both = ("row", "col")

    def shifted(value, target):
        pairs = [(a * cols + b, target(a, b)) for a in range(rows) for b in range(cols)]
        return lax.ppermute(value, both, pairs)

    def by_grid(value, da, db):
        return shifted(value, lambda a, b: ((a + da) % rows) * cols + (b + db) % cols)

    def by_chip(value, k):
        return shifted(value, lambda a, b: (((a // 2 + k) % (rows // 2)) * 2 + a % 2) * cols + b)

    def by_core(value):
        return shifted(value, lambda a, b: (a ^ 1) * cols + b)

    def by_group(value, k):
        return shifted(value, lambda a, b: a * cols + ((b // 4 + k) % 4) * 4 + b % 4)

    def by_member(value, k):
        return shifted(value, lambda a, b: a * cols + (b // 4) * 4 + (b % 4 + k) % 4)

    def exchange(packets):
        east, west, north, south = packets
        from_west = by_grid(east, 0, 1)
        from_east = by_grid(west, 0, -1)
        end = CORNER + FACE
        north = jnp.concatenate([from_west[:CORNER], north, from_east[:CORNER]], axis=0)
        south = jnp.concatenate([from_west[end:], south, from_east[end:]], axis=0)
        from_south = by_grid(north, -1, 0)
        from_north = by_grid(south, 1, 0)
        return from_east, from_west, from_north, from_south

    row, col = lax.axis_index("row"), lax.axis_index("col")
    place = jnp.stack([row // 2, row % 2, col // 4, col % 4]).astype(jnp.int32)

    lists = share_rows[0, 0]
    ids = lax.broadcasted_iota(jnp.int32, lists.shape, 2)
    lists = jnp.where(ids < share_count[0, 0][..., None], lists, -1)
    slots = jnp.concatenate(
        [
            lists[0, 2, :CORNER],
            lists[1, 2],
            lists[2, 2, :CORNER],
            lists[0, 0, :CORNER],
            lists[1, 0],
            lists[2, 0, :CORNER],
            lists[0, 1],
            lists[2, 1],
            jnp.full((NI - SLOTS,), -1, jnp.int32),
        ]
    )[None]

    square = ((NI, NI), BF16)
    to_slots, to_rows, mask, weight, vb, rx, *packets = call(
        order_body,
        [square, square, ((NB, 128), F32), ((1, NI), F32), VEC_B, VEC_X, *PACKETS],
        (slots, mult[0], local_load[0, 0]),
        scratch=[pltpu.VMEM((NI, NI), BF16)],
    )

    def reordered(mat, first, count, scaled):
        return call(
            functools.partial(reorder_body, first, count, scaled),
            [((2, count, NI), BF16)],
            (mat, to_slots, to_rows, weight),
            scratch=[pltpu.VMEM((NI, NI), BF16)] * 2,
        )[0]

    modes_s, tile_s = call(
        small_body,
        [((2, MODES, NI), BF16), ((2, 512, 256), BF16)],
        (modes[0, 0], inverse[0, 0].reshape(256, 512), to_rows, weight),
    )
    arrived = exchange(packets)
    schur_b = reordered(schur[0, 0], 0, NB, False)
    schur_x = reordered(schur[0, 0], NB, NX, False)
    solver_b = reordered(solver[0, 0], 0, NB, True)
    solver_x = reordered(solver[0, 0], NB, NX, True)

    block = ((MODES, RHS), F32)
    rb, rhs = call(first_body, [VEC_B, block], (vb, rx, *arrived, mask, modes_s))
    xb = xx = None
    for step in range(STEPS):
        one, three, two = (by_chip(rhs, k) for k in (1, 3, 2))
        partner = by_core(jnp.concatenate([rhs, one, three, two], axis=0))
        face = ((FACE, RHS), F32)
        keep, *parts = call(
            coarse_body,
            [face] * 4,
            (place, rhs, one, three, two, partner, tile_s),
            scratch=[pltpu.VMEM((256, RHS), F32)],
            smem=1,
        )
        parts = [by_group(v, k) for v, k in zip(parts, (1, 3, 2))]
        own, *parts = call(
            middle_body,
            [block] * 4,
            (place, keep, *parts),
            scratch=[pltpu.VMEM((FACE, RHS), F32)],
            smem=1,
        )
        parts = [by_member(v, k) for v, k in zip(parts, (1, 3, 2))]
        sol, cb, *packets = call(spread_body, [block, VEC_B, *PACKETS], (own, *parts, modes_s))
        cx, pre = call(spread_rest_body, [VEC_X, VEC_B], (sol, modes_s, schur_b))
        arrived = exchange(packets)
        cb, tb, *packets = call(apply_body, [VEC_B, VEC_B, *PACKETS], (cb, *arrived, mask, pre, schur_b))

        def rest(vb, vx, rx, xb, xx, nxt):
            fresh = xb is None
            args = [vb, vx, rx] + ([] if fresh else [xb, xx]) + [schur_x] + ([] if nxt is None else [nxt])
            outs = [VEC_X] + ([] if nxt is None else [((nxt.shape[1], RHS), F32)]) + [VEC_B, VEC_X]

            def body(*refs):
                refs = list(refs)
                vb, vx, rx = refs[:3]
                refs = refs[3:]
                xb = xx = None
                if not fresh:
                    xb, xx = refs[:2]
                    refs = refs[2:]
                mat, refs = refs[0], refs[1:]
                nxt_ref = pre_ref = None
                if nxt is not None:
                    nxt_ref, refs = refs[0], refs[1:]
                rx_out, refs = refs[0], refs[1:]
                if nxt is not None:
                    pre_ref, refs = refs[0], refs[1:]
                apply_rest_body(fresh, vb, vx, rx, xb, xx, mat, nxt_ref, rx_out, pre_ref, *refs)

            got = call(body, outs, args)
            if nxt is None:
                return got[0], None, got[1], got[2]
            return got

        rx, pre, xb, xx = rest(cb, cx, rx, xb, xx, solver_b)
        arrived = exchange(packets)
        rb, gb, *packets = call(solve_body, [VEC_B, VEC_B, *PACKETS], (rb, tb, *arrived, mask, pre, solver_b))
        gx, pre = call(solve_rest_body, [VEC_X, VEC_B], (rb, rx, solver_x, schur_b))
        arrived = exchange(packets)
        ub, tb, *packets = call(apply_body, [VEC_B, VEC_B, *PACKETS], (gb, *arrived, mask, pre, schur_b))
        last = step == STEPS - 1
        rx, pre, xb, xx = rest(ub, gx, rx, xb, xx, None if last else modes_s)
        if last:
            full = ((NI, RHS), F32)
            iterate, pre = call(final_pre_body, [full, full], (xb, xx, rx, to_rows))
        arrived = exchange(packets)
        if last:
            (residual,) = call(final_body, [full], (rb, tb, *arrived, mask, to_rows, pre))
        else:
            rb, rhs = call(close_body, [VEC_B, block], (rb, tb, *arrived, mask, modes_s, pre))
    return iterate[None, None], residual[None, None]


def solution(mesh):
    grid = P("row", "col")
    rows, cols = mesh.shape["row"], mesh.shape["col"]
    return jax.shard_map(
        functools.partial(on_device, rows, cols),
        mesh=mesh,
        in_specs=(grid,) * 8,
        out_specs=(grid, grid),
        check_vma=False,
    )
```

```python
import functools

import jax
import jax.numpy as jnp
from jax import lax
from jax.experimental import pallas as pl
from jax.experimental.pallas import tpu as pltpu
from jax.sharding import PartitionSpec as P

NI = 1024
RHS = 256
MODES = 32
FACE = 128
CORNER = 16
STEPS = 2
BUNDLE = FACE + 2 * CORNER
SIDE = 2 * BUNDLE
NB = 2 * SIDE
F32 = jnp.float32
BF16 = jnp.bfloat16


def dot(a, b):
    return jnp.dot(a, b, preferred_element_type=F32)


def dot_t(a, b):
    return lax.dot_general(a, b, (((0,), (0,)), ((), ())), preferred_element_type=F32)


def split(v):
    high = v.astype(BF16)
    return high, (v - high.astype(F32)).astype(BF16)


def product(mat_high, mat_low, parts, mul=dot):
    high, low = parts
    return mul(mat_high, high) + mul(mat_high, low) + mul(mat_low, high)


def select(onehot, parts):
    high, low = parts
    return dot(onehot, high) + dot(onehot, low)


def call(body, out_shapes, args, scratch=(), smem=0, after=(), limit=16):
    count = len(args)

    def run(*refs):
        return body(*refs[:count], *refs[count + len(after) :])

    specs = [pl.BlockSpec(memory_space=pltpu.SMEM)] * smem
    specs += [pl.BlockSpec(memory_space=pltpu.VMEM)] * (count - smem)
    specs += [pl.BlockSpec(memory_space=pl.ANY)] * len(after)
    return pl.pallas_call(
        run,
        name=getattr(body, "func", body).__name__,
        out_shape=[jax.ShapeDtypeStruct(s, d) for s, d in out_shapes],
        in_specs=specs,
        out_specs=[pl.BlockSpec(memory_space=pltpu.VMEM)] * len(out_shapes),
        scratch_shapes=list(scratch),
        compiler_params=pltpu.CompilerParams(vmem_limit_bytes=limit << 20),
    )(*args, *after)


FULL = ((NI, RHS), F32)
EDGE = ((NB, RHS), F32)
BLOCK = ((MODES, RHS), F32)
FACES = [((FACE, RHS), F32)] * 2
BUNDLES = [((BUNDLE, RHS), F32)] * 2


def put_bundles(v, east, west):
    east[...] = v[:BUNDLE]
    west[...] = v[BUNDLE:]


def put_faces(v, north, south):
    north[...] = v[:FACE]
    south[...] = v[FACE : 2 * FACE]


def received(arrivals):
    from_east, from_west, from_north, from_south = (ref[...] for ref in arrivals)
    end = CORNER + FACE
    return jnp.concatenate(
        [
            from_north[end:],
            from_east[CORNER:end],
            from_south[end:],
            from_north[:CORNER],
            from_west[CORNER:end],
            from_south[:CORNER],
            from_north[CORNER:end],
            from_south[CORNER:end],
            jnp.zeros((NB - SIDE - 2 * FACE, RHS), F32),
        ],
        axis=0,
    )


def as_columns(row, width):
    return jnp.transpose(jnp.broadcast_to(row, (128, width)))


def pick_rows(slots, first, count):
    columns = as_columns(slots.astype(F32), NB)[first : first + count, 0:1]
    lanes = lax.broadcasted_iota(jnp.int32, (count, NI), 1).astype(F32)
    return jnp.where(columns == lanes, 1.0, 0.0).astype(BF16)


def start_body(slots, load, pick_out, east, west):
    pick = pick_rows(slots[...], 0, SIDE)
    pick_out[...] = pick
    put_bundles(select(pick, split(load[...])), east, west)


def start_rest_body(slots, mult, load, modes, tile, pick_out, place_out, weight_out, modes_out, edge_modes_out, tile_out, pre_out, north, south):
    pick = pick_rows(slots[...], SIDE, SIDE)
    pick_out[...] = pick
    parts = split(load[...])
    put_faces(select(pick, parts), north, south)
    key = slots[...]
    for blk in range(8):
        rows = lax.broadcasted_iota(jnp.int32, (128, NB), 0) + 128 * blk
        place_out[128 * blk : 128 * (blk + 1), :] = jnp.where(rows == key, 1.0, 0.0).astype(BF16)
    weight = 1.0 / mult[...].astype(F32)
    weight_out[...] = as_columns(weight, NI)
    high, low = split(modes[...] * weight)
    modes_out[0] = high
    modes_out[1] = low
    edge_modes_out[0] = dot(high, place_out[...]).astype(BF16)
    edge_modes_out[1] = dot(low, place_out[...]).astype(BF16)
    pre_out[...] = product(high, low, parts)
    a, b = split(jnp.transpose(tile[...]))
    tile_out[0] = a
    tile_out[1] = b


def matrix_body(scaled, *refs):
    mat, pick_ew, pick_ns = refs[:3]
    full, edge = refs[-2:]
    for blk in range(4):
        rows = slice(256 * blk, 256 * (blk + 1))
        value = mat[rows, :]
        if scaled:
            mult, column = refs[3:5]
            value = value * (1.0 / mult[...].astype(F32)) * column[rows, 0:1]
        a, b = split(value)
        full[0, rows, :] = a
        full[1, rows, :] = b
    for level in range(2):
        edge[level, :SIDE, :] = dot(pick_ew[...], full[level]).astype(BF16)
        edge[level, SIDE:, :] = dot(pick_ns[...], full[level]).astype(BF16)


def corner_body(edge, place, out):
    for level in range(2):
        out[level] = dot(edge[level], place[...]).astype(BF16)


def first_body(fe, fw, fn, fs, pre, edge_modes, edge_out, rhs_out):
    edge = received((fe, fw, fn, fs))
    edge_out[...] = edge
    rhs_out[...] = pre[...] + product(edge_modes[0], edge_modes[1], split(edge))


def close_body(fe, fw, fn, fs, pre, edge_modes, edge_out, rhs_out):
    edge = received((fe, fw, fn, fs))
    edge_out[...] = edge
    rhs_out[...] = pre[...] - product(edge_modes[0], edge_modes[1], split(edge))


def first_rest_body(load, edge, place, r_out):
    r_out[...] = load[...] + select(place[...], split(edge[...]))


def close_rest_body(mid, edge, place, r_out):
    r_out[...] = mid[...] - select(place[...], split(edge[...]))


def final_body(mid, fe, fw, fn, fs, place, r_out):
    r_out[...] = mid[...] - select(place[...], split(received((fe, fw, fn, fs))))


def coarse_body(position, own, one, three, two, partner, tile, keep, out_one, out_three, out_two, gathered):
    chip, core, group = position[0], position[1], position[2]
    for side in range(2):
        which = core if side == 0 else 1 - core
        for slot, (ref, shift) in enumerate(((own, 0), (one, 1), (three, 3), (two, 2))):
            block = 2 * lax.rem(chip + 4 - shift, 4) + which
            value = ref[...] if side == 0 else partner[slot * MODES : (slot + 1) * MODES]
            gathered[pl.ds(pl.multiple_of(block * MODES, MODES), MODES), :] = value
    parts = split(gathered[...])
    for ref, shift in ((out_one, 1), (out_three, 3), (out_two, 2), (keep, 0)):
        rows = pl.ds(pl.multiple_of(lax.rem(group + shift, 4) * FACE, FACE), FACE)
        ref[...] = product(tile[0, rows, :], tile[1, rows, :], parts)


def middle_body(position, keep, one, three, two, own, out_one, out_three, out_two, total):
    member = position[3]
    total[...] = (keep[...] + one[...]) + (three[...] + two[...])
    for ref, shift in ((own, 0), (out_one, 1), (out_three, 3), (out_two, 2)):
        rows = pl.ds(pl.multiple_of(lax.rem(member + shift, 4) * MODES, MODES), MODES)
        ref[...] = total[rows, :]


def spread_body(own, one, three, two, edge_modes, sol_out, east, west):
    sol = (own[...] + one[...]) + (three[...] + two[...])
    sol_out[...] = sol
    put_bundles(product(edge_modes[0, :, :SIDE], edge_modes[1, :, :SIDE], split(sol), dot_t), east, west)


def spread_rest_body(sol, modes, edge_modes, schur_edge, c_out, pre_out, north, south):
    parts = split(sol[...])
    put_faces(product(edge_modes[0, :, SIDE:], edge_modes[1, :, SIDE:], parts, dot_t), north, south)
    c = product(modes[0], modes[1], parts, dot_t)
    c_out[...] = c
    pre_out[...] = product(schur_edge[0], schur_edge[1], split(c))


def apply_body(sign, fe, fw, fn, fs, pre, corner, edge_out, east, west):
    edge = received((fe, fw, fn, fs))
    edge_out[...] = edge
    t = product(corner[0, :SIDE, :], corner[1, :SIDE, :], split(edge))
    put_bundles(pre[:SIDE, :] + t if sign > 0 else pre[:SIDE, :] - t, east, west)


def apply_rest_body(fresh, last, *refs):
    edge, local, r, pre, place, full, corner = refs[:7]
    refs = refs[7:]
    if not last:
        nxt, refs = refs[0], refs[1:]
    if not fresh:
        x, refs = refs[0], refs[1:]
    if last:
        mid_out, x_out, north, south = refs
    else:
        mid_out, x_out, pre_out, north, south = refs
    parts = split(edge[...])
    put_faces(pre[SIDE:, :] + product(corner[0, SIDE:, :], corner[1, SIDE:, :], parts), north, south)
    v = local[...] + select(place[...], parts)
    x_out[...] = v if fresh else x[...] + v
    mid = r[...] - product(full[0], full[1], split(v))
    mid_out[...] = mid
    if not last:
        pre_out[...] = product(nxt[0], nxt[1], split(mid))


def solve_rest_body(edge, mid, pre, place, full, corner, nxt, r_out, g_out, pre_out, north, south):
    parts = split(edge[...])
    put_faces(pre[SIDE:, :] - product(corner[0, SIDE:, :], corner[1, SIDE:, :], parts), north, south)
    r = mid[...] - select(place[...], parts)
    r_out[...] = r
    g = product(full[0], full[1], split(r))
    g_out[...] = g
    pre_out[...] = product(nxt[0], nxt[1], split(g))


def on_device(rows, cols, local_load, schur, solver, modes, inverse, share_rows, share_count, mult):
    both = ("row", "col")

    def shifted(value, target):
        pairs = [(a * cols + b, target(a, b)) for a in range(rows) for b in range(cols)]
        return lax.ppermute(value, both, pairs)

    def by_grid(value, da, db):
        return shifted(value, lambda a, b: ((a + da) % rows) * cols + (b + db) % cols)

    def by_chip(value, k):
        return shifted(value, lambda a, b: (((a // 2 + k) % (rows // 2)) * 2 + a % 2) * cols + b)

    def by_core(value):
        return shifted(value, lambda a, b: (a ^ 1) * cols + b)

    def by_group(value, k):
        return shifted(value, lambda a, b: a * cols + ((b // 4 + k) % 4) * 4 + b % 4)

    def by_member(value, k):
        return shifted(value, lambda a, b: a * cols + (b // 4) * 4 + (b % 4 + k) % 4)

    def sideways(east, west):
        return by_grid(west, 0, -1), by_grid(east, 0, 1)

    def across(arrived, north, south):
        from_east, from_west = arrived
        end = CORNER + FACE
        north = jnp.concatenate([from_west[:CORNER], north, from_east[:CORNER]], axis=0)
        south = jnp.concatenate([from_west[end:], south, from_east[end:]], axis=0)
        return from_east, from_west, by_grid(south, 1, 0), by_grid(north, -1, 0)

    row, col = lax.axis_index("row"), lax.axis_index("col")
    position = jnp.stack([row // 2, row % 2, col // 4, col % 4]).astype(jnp.int32)

    lists = share_rows[0, 0]
    ids = lax.broadcasted_iota(jnp.int32, lists.shape, 2)
    lists = jnp.where(ids < share_count[0, 0][..., None], lists, -1)
    slots = jnp.concatenate(
        [
            lists[0, 2, :CORNER],
            lists[1, 2],
            lists[2, 2, :CORNER],
            lists[0, 0, :CORNER],
            lists[1, 0],
            lists[2, 0, :CORNER],
            lists[0, 1],
            lists[2, 1],
            jnp.full((NB - SIDE - 2 * FACE,), -1, jnp.int32),
        ]
    )[None]
    load = local_load[0, 0]

    half_pick = ((SIDE, NI), BF16)
    pick_ew, *packets = call(start_body, [half_pick, *BUNDLES], (slots, load))
    arrived = sideways(*packets)
    pick_ns, place, weight, modes_s, edge_modes, tile, pre, *faces = call(
        start_rest_body,
        [
            half_pick,
            ((NI, NB), BF16),
            ((NI, 128), F32),
            ((2, MODES, NI), BF16),
            ((2, MODES, NB), BF16),
            ((2, 512, 256), BF16),
            BLOCK,
            *FACES,
        ],
        (slots, mult[0], load, modes[0, 0], inverse[0, 0].reshape(256, 512)),
    )
    arrived = across(arrived, *faces)

    matrices = [((2, NI, NI), BF16), ((2, NB, NI), BF16)]
    corner_shape = [((2, NB, NB), BF16)]
    schur_full, schur_edge = call(
        functools.partial(matrix_body, False), matrices, (schur[0, 0], pick_ew, pick_ns), limit=24
    )
    (schur_corner,) = call(corner_body, corner_shape, (schur_edge, place))

    edge, rhs = call(first_body, [EDGE, BLOCK], (*arrived, pre, edge_modes), after=(schur_edge,))
    x = mid = None
    for step in range(STEPS):
        one, three, two = (by_chip(rhs, k) for k in (1, 3, 2))
        if step == 0:
            (r,) = call(first_rest_body, [FULL], (load, edge, place))
        else:
            (r,) = call(close_rest_body, [FULL], (mid, edge, place))
        partner = by_core(jnp.concatenate([rhs, one, three, two], axis=0))
        face = ((FACE, RHS), F32)
        keep, *parts = call(
            coarse_body,
            [face] * 4,
            (position, rhs, one, three, two, partner, tile),
            scratch=[pltpu.VMEM((256, RHS), F32)],
            smem=1,
            after=(r, schur_corner) if step == 0 else (r,),
        )
        if step == 0:
            solver_full, solver_edge = call(
                functools.partial(matrix_body, True),
                matrices,
                (solver[0, 0], pick_ew, pick_ns, mult[0], weight),
                after=(keep,),
                limit=24,
            )
        parts = [by_group(v, k) for v, k in zip(parts, (1, 3, 2))]
        own, *parts = call(
            middle_body,
            [BLOCK] * 4,
            (position, keep, *parts),
            scratch=[pltpu.VMEM((FACE, RHS), F32)],
            smem=1,
            after=(solver_edge,) if step == 0 else (),
        )
        if step == 0:
            (solver_corner,) = call(corner_body, corner_shape, (solver_edge, place), after=(own,))
        parts = [by_member(v, k) for v, k in zip(parts, (1, 3, 2))]
        sol, *packets = call(
            spread_body,
            [BLOCK, *BUNDLES],
            (own, *parts, edge_modes),
            after=(solver_corner,) if step == 0 else (),
        )
        arrived = sideways(*packets)
        c, pre, *faces = call(spread_rest_body, [FULL, EDGE, *FACES], (sol, modes_s, edge_modes, schur_edge))
        arrived = across(arrived, *faces)

        def apply(arrived, pre, local, r, x, nxt):
            edge, *packets = call(
                functools.partial(apply_body, 1), [EDGE, *BUNDLES], (*arrived, pre, schur_corner)
            )
            arrived = sideways(*packets)
            fresh, last = x is None, nxt is None
            args = [edge, local, r, pre, place, schur_full, schur_corner]
            args += ([] if last else [nxt]) + ([] if fresh else [x])
            outs = [FULL, FULL] + ([] if last else [((nxt.shape[1], RHS), F32)]) + FACES
            mid, x, *got = call(functools.partial(apply_rest_body, fresh, last), outs, args)
            pre = None if last else got[0]
            return across(arrived, *got[-2:]), mid, x, pre

        arrived, mid, x, pre = apply(arrived, pre, c, r, x, solver_edge)

        edge, *packets = call(functools.partial(apply_body, -1), [EDGE, *BUNDLES], (*arrived, pre, solver_corner))
        arrived = sideways(*packets)
        r, g, pre, *faces = call(
            solve_rest_body,
            [FULL, FULL, EDGE, *FACES],
            (edge, mid, pre, place, solver_full, solver_corner, schur_edge),
        )
        arrived = across(arrived, *faces)

        last = step == STEPS - 1
        arrived, mid, x, pre = apply(arrived, pre, g, r, x, None if last else modes_s)
        if last:
            (residual,) = call(final_body, [FULL], (mid, *arrived, place))
        else:
            edge, rhs = call(close_body, [EDGE, BLOCK], (*arrived, pre, edge_modes))
    return x[None, None], residual[None, None]


def solution(mesh):
    grid = P("row", "col")
    rows, cols = mesh.shape["row"], mesh.shape["col"]
    return jax.shard_map(
        functools.partial(on_device, rows, cols),
        mesh=mesh,
        in_specs=(grid,) * 8,
        out_specs=(grid, grid),
        check_vma=False,
    )
```

```python
import functools

import jax
import jax.numpy as jnp
from jax import lax
from jax.experimental import pallas as pl
from jax.experimental.pallas import tpu as pltpu
from jax.sharding import PartitionSpec as P

NI = 1024
RHS = 256
MODES = 32
FACE = 128
CORNER = 16
STEPS = 2
BUNDLE = FACE + 2 * CORNER
SIDE = 2 * BUNDLE
NB = 2 * SIDE
F32 = jnp.float32
BF16 = jnp.bfloat16


def dot(a, b):
    return jnp.dot(a, b, preferred_element_type=F32)


def dot_t(a, b):
    return lax.dot_general(a, b, (((0,), (0,)), ((), ())), preferred_element_type=F32)


def split(v):
    high = v.astype(BF16)
    return high, (v - high.astype(F32)).astype(BF16)


def product(mat_high, mat_low, parts, mul=dot):
    high, low = parts
    return mul(mat_high, high) + mul(mat_high, low) + mul(mat_low, high)


def select(onehot, parts):
    high, low = parts
    return dot(onehot, high) + dot(onehot, low)


def call(body, out_shapes, args, scratch=(), smem=0, after=(), limit=4):
    count = len(args)

    def run(*refs):
        return body(*refs[:count], *refs[count + len(after) :])

    specs = [pl.BlockSpec(memory_space=pltpu.SMEM)] * smem
    specs += [pl.BlockSpec(memory_space=pltpu.VMEM)] * (count - smem)
    specs += [pl.BlockSpec(memory_space=pltpu.VMEM)] * len(after)
    return pl.pallas_call(
        run,
        name=getattr(body, "func", body).__name__,
        out_shape=[jax.ShapeDtypeStruct(s, d) for s, d in out_shapes],
        in_specs=specs,
        out_specs=[pl.BlockSpec(memory_space=pltpu.VMEM)] * len(out_shapes),
        scratch_shapes=list(scratch),
        compiler_params=pltpu.CompilerParams(vmem_limit_bytes=limit << 20),
    )(*args, *after)


FULL = ((NI, RHS), F32)
EDGE = ((NB, RHS), F32)
BLOCK = ((MODES, RHS), F32)
FACES = [((FACE, RHS), F32)] * 2
BUNDLES = [((BUNDLE, RHS), F32)] * 2


def put_bundles(v, east, west):
    east[...] = v[:BUNDLE]
    west[...] = v[BUNDLE:]


def put_faces(v, north, south):
    north[...] = v[:FACE]
    south[...] = v[FACE : 2 * FACE]


def received(arrivals):
    side0, side1, cross0, cross1 = (ref[...] for ref in arrivals)
    end = CORNER + FACE
    return jnp.concatenate(
        [
            cross0[:CORNER],
            side0[CORNER:end],
            cross1[:CORNER],
            cross0[end:],
            side1[CORNER:end],
            cross1[end:],
            cross0[CORNER:end],
            cross1[CORNER:end],
            jnp.zeros((NB - SIDE - 2 * FACE, RHS), F32),
        ],
        axis=0,
    )


def as_columns(row, width):
    return jnp.transpose(jnp.broadcast_to(row, (128, width)))


def pick_rows(slots, first, count):
    columns = as_columns(slots.astype(F32), NB)[first : first + count, 0:1]
    lanes = lax.broadcasted_iota(jnp.int32, (count, NI), 1).astype(F32)
    return jnp.where(columns == lanes, 1.0, 0.0).astype(BF16)


def start_body(slots, load, pick_out, east, west):
    pick = pick_rows(slots[...], 0, SIDE)
    pick_out[...] = pick
    put_bundles(select(pick, split(load[...])), east, west)


def start_rest_body(slots, mult, load, modes, tile, pick_out, place_out, weight_out, modes_out, edge_modes_out, tile_out, pre_out, north, south):
    pick = pick_rows(slots[...], SIDE, SIDE)
    pick_out[...] = pick
    parts = split(load[...])
    put_faces(select(pick, parts), north, south)
    key = slots[...]
    for blk in range(8):
        rows = lax.broadcasted_iota(jnp.int32, (128, NB), 0) + 128 * blk
        place_out[128 * blk : 128 * (blk + 1), :] = jnp.where(rows == key, 1.0, 0.0).astype(BF16)
    weight = 1.0 / mult[...].astype(F32)
    weight_out[...] = as_columns(weight, NI)
    high, low = split(modes[...] * weight)
    modes_out[0] = high
    modes_out[1] = low
    edge_modes_out[0] = dot(high, place_out[...]).astype(BF16)
    edge_modes_out[1] = dot(low, place_out[...]).astype(BF16)
    pre_out[...] = product(high, low, parts)
    a, b = split(jnp.transpose(tile[...]))
    tile_out[0] = a
    tile_out[1] = b


def matrix_body(scaled, *refs):
    mat, pick_ew, pick_ns = refs[:3]
    full, edge, token = refs[-3:]
    token[...] = jnp.zeros_like(token)
    for blk in range(4):
        rows = slice(256 * blk, 256 * (blk + 1))
        value = mat[rows, :]
        if scaled:
            mult, column = refs[3:5]
            value = value * (1.0 / mult[...].astype(F32)) * column[rows, 0:1]
        a, b = split(value)
        full[0, rows, :] = a
        full[1, rows, :] = b
    for level in range(2):
        edge[level, :SIDE, :] = dot(pick_ew[...], full[level]).astype(BF16)
        edge[level, SIDE:, :] = dot(pick_ns[...], full[level]).astype(BF16)


def corner_body(edge, place, out, token):
    token[...] = jnp.zeros_like(token)
    for level in range(2):
        out[level] = dot(edge[level], place[...]).astype(BF16)


def first_body(fe, fw, fn, fs, pre, edge_modes, edge_out, rhs_out):
    edge = received((fe, fw, fn, fs))
    edge_out[...] = edge
    rhs_out[...] = pre[...] + product(edge_modes[0], edge_modes[1], split(edge))


def close_body(fe, fw, fn, fs, pre, edge_modes, edge_out, rhs_out):
    edge = received((fe, fw, fn, fs))
    edge_out[...] = edge
    rhs_out[...] = pre[...] - product(edge_modes[0], edge_modes[1], split(edge))


def first_rest_body(load, edge, place, r_out):
    r_out[...] = load[...] + select(place[...], split(edge[...]))


def close_rest_body(mid, edge, place, r_out):
    r_out[...] = mid[...] - select(place[...], split(edge[...]))


def final_body(mid, fe, fw, fn, fs, place, r_out):
    r_out[...] = mid[...] - select(place[...], split(received((fe, fw, fn, fs))))


def coarse_body(position, own, one, three, two, partner, tile, keep, out_one, out_three, out_two, gathered):
    chip, core, group = position[0], position[1], position[2]
    for side in range(2):
        which = core if side == 0 else 1 - core
        for slot, (ref, shift) in enumerate(((own, 0), (one, 1), (three, 3), (two, 2))):
            block = 2 * lax.rem(chip + 4 - shift, 4) + which
            value = ref[...] if side == 0 else partner[slot * MODES : (slot + 1) * MODES]
            gathered[pl.ds(pl.multiple_of(block * MODES, MODES), MODES), :] = value
    parts = split(gathered[...])
    for ref, shift in ((out_one, 1), (out_three, 3), (out_two, 2), (keep, 0)):
        rows = pl.ds(pl.multiple_of(lax.rem(group + shift, 4) * FACE, FACE), FACE)
        ref[...] = product(tile[0, rows, :], tile[1, rows, :], parts)


def middle_body(position, keep, one, three, two, own, out_one, out_three, out_two, total):
    member = position[3]
    total[...] = (keep[...] + one[...]) + (three[...] + two[...])
    for ref, shift in ((own, 0), (out_one, 1), (out_three, 3), (out_two, 2)):
        rows = pl.ds(pl.multiple_of(lax.rem(member + shift, 4) * MODES, MODES), MODES)
        ref[...] = total[rows, :]


def spread_body(own, one, three, two, edge_modes, sol_out, east, west):
    sol = (own[...] + one[...]) + (three[...] + two[...])
    sol_out[...] = sol
    put_bundles(product(edge_modes[0, :, :SIDE], edge_modes[1, :, :SIDE], split(sol), dot_t), east, west)


def spread_rest_body(sol, modes, edge_modes, c_out, north, south):
    parts = split(sol[...])
    put_faces(product(edge_modes[0, :, SIDE:], edge_modes[1, :, SIDE:], parts, dot_t), north, south)
    c_out[...] = product(modes[0], modes[1], parts, dot_t)


def apply_body(sign, fe, fw, fn, fs, pre, corner, edge_out, east, west):
    edge = received((fe, fw, fn, fs))
    edge_out[...] = edge
    t = product(corner[0, :SIDE, :], corner[1, :SIDE, :], split(edge))
    put_bundles(pre[:SIDE, :] + t if sign > 0 else pre[:SIDE, :] - t, east, west)


def apply_rest_body(fresh, *refs):
    edge, local, r, pre, place, full, corner = refs[:7]
    mid_out, x_out, north, south = refs[-4:]
    parts = split(edge[...])
    put_faces(pre[SIDE:, :] + product(corner[0, SIDE:, :], corner[1, SIDE:, :], parts), north, south)
    v = local[...] + select(place[...], parts)
    x_out[...] = v if fresh else refs[7][...] + v
    mid_out[...] = r[...] - product(full[0], full[1], split(v))


def solve_rest_body(edge, mid, pre, place, full, corner, r_out, g_out, north, south):
    parts = split(edge[...])
    put_faces(pre[SIDE:, :] - product(corner[0, SIDE:, :], corner[1, SIDE:, :], parts), north, south)
    r = mid[...] - select(place[...], parts)
    r_out[...] = r
    g_out[...] = product(full[0], full[1], split(r))


def local_body(mat, v, out):
    out[...] = product(mat[0], mat[1], split(v[...]))


def on_device(rows, cols, local_load, schur, solver, modes, inverse, share_rows, share_count, mult):
    both = ("row", "col")

    def shifted(value, target):
        pairs = [(a * cols + b, target(a, b)) for a in range(rows) for b in range(cols)]
        return lax.ppermute(value, both, pairs)

    def partner_of(i, k, count):
        return (((i + k) ^ 1) - k) % count

    def by_col(value, k):
        return shifted(value, lambda a, b: a * cols + partner_of(b, k, cols))

    def by_row(value, k):
        return shifted(value, lambda a, b: partner_of(a, k, rows) * cols + b)

    def by_chip(value, k):
        return shifted(value, lambda a, b: (((a // 2 + k) % (rows // 2)) * 2 + a % 2) * cols + b)

    def by_core(value):
        return shifted(value, lambda a, b: (a ^ 1) * cols + b)

    def by_group(value, k):
        return shifted(value, lambda a, b: a * cols + ((b // 4 + k) % 4) * 4 + b % 4)

    def by_member(value, k):
        return shifted(value, lambda a, b: a * cols + (b // 4) * 4 + (b % 4 + k) % 4)

    def sideways(side0, side1):
        return by_col(side0, 0), by_col(side1, 1)

    def across(arrived, face0, face1):
        side0, side1 = arrived
        end = CORNER + FACE
        cross0 = jnp.concatenate([side0[:CORNER], face0, side1[:CORNER]], axis=0)
        cross1 = jnp.concatenate([side0[end:], face1, side1[end:]], axis=0)
        return side0, side1, by_row(cross0, 0), by_row(cross1, 1)

    def local(mat, v):
        return call(local_body, [((mat.shape[1], RHS), F32)], (mat, v))[0]

    row, col = lax.axis_index("row"), lax.axis_index("col")
    position = jnp.stack([row // 2, row % 2, col // 4, col % 4]).astype(jnp.int32)

    lists = share_rows[0, 0]
    ids = lax.broadcasted_iota(jnp.int32, lists.shape, 2)
    lists = jnp.where(ids < share_count[0, 0][..., None], lists, -1)
    lists = jnp.where(row % 2 == 1, lists[::-1], lists)
    lists = jnp.where(col % 2 == 1, lists[:, ::-1], lists)
    slots = jnp.concatenate(
        [
            lists[2, 2, :CORNER],
            lists[1, 2],
            lists[0, 2, :CORNER],
            lists[2, 0, :CORNER],
            lists[1, 0],
            lists[0, 0, :CORNER],
            lists[2, 1],
            lists[0, 1],
            jnp.full((NB - SIDE - 2 * FACE,), -1, jnp.int32),
        ]
    )[None]
    load = local_load[0, 0]

    half_pick = ((SIDE, NI), BF16)
    pick_ew, *packets = call(start_body, [half_pick, *BUNDLES], (slots, load))
    arrived = sideways(*packets)
    pick_ns, place, weight, modes_s, edge_modes, tile, pre, *faces = call(
        start_rest_body,
        [
            half_pick,
            ((NI, NB), BF16),
            ((NI, 128), F32),
            ((2, MODES, NI), BF16),
            ((2, MODES, NB), BF16),
            ((2, 512, 256), BF16),
            BLOCK,
            *FACES,
        ],
        (slots, mult[0], load, modes[0, 0], inverse[0, 0].reshape(256, 512)),
    )
    arrived = across(arrived, *faces)

    token = ((8, 128), F32)
    matrices = [((2, NI, NI), BF16), ((2, NB, NI), BF16), token]
    corner_shape = [((2, NB, NB), BF16), token]
    schur_full, schur_edge, schur_token = call(
        functools.partial(matrix_body, False), matrices, (schur[0, 0], pick_ew, pick_ns)
    )
    schur_corner, corner_token = call(corner_body, corner_shape, (schur_edge, place))

    edge, rhs = call(first_body, [EDGE, BLOCK], (*arrived, pre, edge_modes), after=(schur_token,))
    x = mid = None
    for step in range(STEPS):
        one, three, two = (by_chip(rhs, k) for k in (1, 3, 2))
        if step == 0:
            (r,) = call(first_rest_body, [FULL], (load, edge, place))
        else:
            (r,) = call(close_rest_body, [FULL], (mid, edge, place))
        partner = by_core(jnp.concatenate([rhs, one, three, two], axis=0))
        face = ((FACE, RHS), F32)
        keep, *parts = call(
            coarse_body,
            [face] * 4,
            (position, rhs, one, three, two, partner, tile),
            scratch=[pltpu.VMEM((256, RHS), F32)],
            smem=1,
            after=(r, corner_token) if step == 0 else (r,),
        )
        if step == 0:
            solver_full, solver_edge, solver_token = call(
                functools.partial(matrix_body, True),
                matrices,
                (solver[0, 0], pick_ew, pick_ns, mult[0], weight),
                after=(keep,),
            )
        parts = [by_group(v, k) for v, k in zip(parts, (1, 3, 2))]
        own, *parts = call(
            middle_body,
            [BLOCK] * 4,
            (position, keep, *parts),
            scratch=[pltpu.VMEM((FACE, RHS), F32)],
            smem=1,
            after=(solver_token,) if step == 0 else (),
        )
        if step == 0:
            solver_corner, corner_token = call(corner_body, corner_shape, (solver_edge, place), after=(own,))
        parts = [by_member(v, k) for v, k in zip(parts, (1, 3, 2))]
        sol, *packets = call(
            spread_body,
            [BLOCK, *BUNDLES],
            (own, *parts, edge_modes),
            after=(corner_token,) if step == 0 else (),
        )
        arrived = sideways(*packets)
        c, *faces = call(spread_rest_body, [FULL, *FACES], (sol, modes_s, edge_modes))
        pre = local(schur_edge, c)
        arrived = across(arrived, *faces)

        def apply(arrived, pre, v, r, x):
            edge, *packets = call(
                functools.partial(apply_body, 1), [EDGE, *BUNDLES], (*arrived, pre, schur_corner)
            )
            arrived = sideways(*packets)
            fresh = x is None
            args = [edge, v, r, pre, place, schur_full, schur_corner] + ([] if fresh else [x])
            mid, x, *faces = call(functools.partial(apply_rest_body, fresh), [FULL, FULL, *FACES], args)
            return across(arrived, *faces), mid, x

        arrived, mid, x = apply(arrived, pre, c, r, x)
        pre = local(solver_edge, mid)

        edge, *packets = call(functools.partial(apply_body, -1), [EDGE, *BUNDLES], (*arrived, pre, solver_corner))
        arrived = sideways(*packets)
        r, g, *faces = call(
            solve_rest_body, [FULL, FULL, *FACES], (edge, mid, pre, place, solver_full, solver_corner)
        )
        arrived = across(arrived, *faces)
        pre = local(schur_edge, g)

        last = step == STEPS - 1
        arrived, mid, x = apply(arrived, pre, g, r, x)
        if last:
            (residual,) = call(final_body, [FULL], (mid, *arrived, place))
        else:
            pre = local(modes_s, mid)
            edge, rhs = call(close_body, [EDGE, BLOCK], (*arrived, pre, edge_modes))
    return x[None, None], residual[None, None]


def solution(mesh):
    grid = P("row", "col")
    rows, cols = mesh.shape["row"], mesh.shape["col"]
    return jax.shard_map(
        functools.partial(on_device, rows, cols),
        mesh=mesh,
        in_specs=(grid,) * 8,
        out_specs=(grid, grid),
        check_vma=False,
    )
```

```python
import functools

import jax
import jax.numpy as jnp
from jax import lax
from jax.experimental import pallas as pl
from jax.experimental.pallas import tpu as pltpu
from jax.sharding import PartitionSpec as P

NI = 1024
RHS = 256
MODES = 32
FACE = 128
CORNER = 16
STEPS = 2
BUNDLE = FACE + 2 * CORNER
SIDE = 2 * BUNDLE
NB = 2 * SIDE
F32 = jnp.float32
BF16 = jnp.bfloat16


def dot(a, b):
    return jnp.dot(a, b, preferred_element_type=F32)


def dot_t(a, b):
    return lax.dot_general(a, b, (((0,), (0,)), ((), ())), preferred_element_type=F32)


def split(v):
    high = v.astype(BF16)
    return high, (v - high.astype(F32)).astype(BF16)


def product(mat_high, mat_low, parts, mul=dot):
    high, low = parts
    return mul(mat_high, high) + mul(mat_high, low) + mul(mat_low, high)


def select(onehot, parts):
    high, low = parts
    return dot(onehot, high) + dot(onehot, low)


def half_of(i, count):
    size = count // 2 if count > FACE else count
    parts = count // size
    return lax.div(i, parts), pl.ds(pl.multiple_of(lax.rem(i, parts) * size, size), size), parts


def add_product(out, mat, parts, sign):
    count = mat.shape[1]

    def once(i, carry):
        level, rows, _ = half_of(i, count)
        t = dot(mat[lax.div(level, 2), rows, :], parts[lax.rem(level, 2)])
        out[rows, :] = out[rows, :] + t if sign > 0 else out[rows, :] - t
        return carry

    lax.fori_loop(0, 3 * half_of(0, count)[2], once, 0)


def add_select(out, onehot, parts, sign):
    count = onehot.shape[0]

    def once(i, carry):
        level, rows, _ = half_of(i, count)
        t = dot(onehot[rows, :], parts[level])
        out[rows, :] = out[rows, :] + t if sign > 0 else out[rows, :] - t
        return carry

    lax.fori_loop(0, 2 * half_of(0, count)[2], once, 0)


def keep_halves(parts, v):
    def step(rows):
        parts[0, rows, :], parts[1, rows, :] = split(v[rows, :])

    by_rows(v.shape[0], min(v.shape[0], 128), step)


def fill(out, value):
    def step(rows):
        out[rows, :] = jnp.zeros((rows.size, RHS), F32) if value is None else value[rows, :]

    by_rows(out.shape[0], min(out.shape[0], 128), step)


def by_rows(count, size, step):
    def once(i, carry):
        step(pl.ds(pl.multiple_of(i * size, size), size))
        return carry

    lax.fori_loop(0, count // size, once, 0)


def call(body, out_shapes, args, scratch=(), smem=0, after=(), limit=6):
    count = len(args)

    def run(*refs):
        return body(*refs[:count], *refs[count + len(after) :])

    specs = [pl.BlockSpec(memory_space=pltpu.SMEM)] * smem
    specs += [pl.BlockSpec(memory_space=pltpu.VMEM)] * (count - smem)
    specs += [pl.BlockSpec(memory_space=pltpu.VMEM)] * len(after)
    return pl.pallas_call(
        run,
        name=getattr(body, "func", body).__name__,
        out_shape=[jax.ShapeDtypeStruct(s, d) for s, d in out_shapes],
        in_specs=specs,
        out_specs=[pl.BlockSpec(memory_space=pltpu.VMEM)] * len(out_shapes),
        scratch_shapes=list(scratch),
        compiler_params=pltpu.CompilerParams(vmem_limit_bytes=limit << 20),
    )(*args, *after)


PARTS = pltpu.VMEM((2, NI, RHS), BF16)
EDGE_PARTS = pltpu.VMEM((2, NB, RHS), BF16)
EDGE_SCRATCH = [pltpu.VMEM((NB, RHS), F32), EDGE_PARTS]
FULL = ((NI, RHS), F32)
EDGE = ((NB, RHS), F32)
BLOCK = ((MODES, RHS), F32)
TOKEN = ((8, 128), F32)
FACES = [((FACE, RHS), F32)] * 2
BUNDLES = [((BUNDLE, RHS), F32)] * 2
PACKETS = BUNDLES + FACES


def put_packets(v, side0, side1, face0, face1):
    side0[...] = v[:BUNDLE]
    side1[...] = v[BUNDLE:SIDE]
    face0[...] = v[SIDE : SIDE + FACE]
    face1[...] = v[SIDE + FACE : SIDE + 2 * FACE]


def received(arrivals):
    side0, side1, face0, face1, corner0, corner1 = (ref[...] for ref in arrivals)
    end = CORNER + FACE
    return jnp.concatenate(
        [
            corner0[:CORNER],
            side0[CORNER:end],
            corner1[:CORNER],
            corner0[CORNER:],
            side1[CORNER:end],
            corner1[CORNER:],
            face0,
            face1,
            jnp.zeros((NB - SIDE - 2 * FACE, RHS), F32),
        ],
        axis=0,
    )


def turn_body(side0, side1, corner0, corner1):
    end = CORNER + FACE
    corner0[...] = jnp.concatenate([side0[:CORNER], side1[:CORNER]], axis=0)
    corner1[...] = jnp.concatenate([side0[end:], side1[end:]], axis=0)


def as_columns(row, width):
    return jnp.transpose(jnp.broadcast_to(row, (128, width)))


def pick_rows(lists, counts, order):
    turn_row, turn_col = lax.rem(lax.axis_index("row"), 2), lax.rem(lax.axis_index("col"), 2)
    blocks = []
    for p, q, size in order:
        a = p if p == 1 else p + 2 * (1 - p) * turn_row
        b = q if q == 1 else q + 2 * (1 - q) * turn_col
        ids = lax.broadcasted_iota(jnp.int32, (1, FACE), 1)
        row = jnp.where(ids < counts[a, b], lists[a, pl.ds(b, 1), :], -1).astype(F32)
        column = as_columns(row, FACE)[:size, 0:1]
        lanes = lax.broadcasted_iota(jnp.int32, (size, NI), 1).astype(F32)
        blocks.append(jnp.where(column == lanes, 1.0, 0.0))
    return blocks


SIDE_LISTS = (
    (2, 2, CORNER),
    (1, 2, FACE),
    (0, 2, CORNER),
    (2, 0, CORNER),
    (1, 0, FACE),
    (0, 0, CORNER),
)
FACE_LISTS = ((2, 1, FACE), (0, 1, FACE))


def start_body(counts, lists, load, pick_out, side0, side1):
    pick = jnp.concatenate(pick_rows(lists, counts, SIDE_LISTS), axis=0).astype(BF16)
    pick_out[...] = pick
    v = select(pick, split(load[...]))
    side0[...] = v[:BUNDLE]
    side1[...] = v[BUNDLE:]


def start_rest_body(counts, lists, pick_ew, mult, load, modes, tile, pick_out, place_out, weight_out, modes_out, edge_modes_out, tile_out, pre_out, face0, face1):
    rest = pick_rows(lists, counts, FACE_LISTS)
    pick = jnp.concatenate(rest + [jnp.zeros((NB - SIDE - 2 * FACE, NI), F32)], axis=0)
    pick_out[...] = pick.astype(BF16)
    parts = split(load[...])
    v = select(pick_out[: 2 * FACE, :], parts)
    face0[...] = v[:FACE]
    face1[...] = v[FACE:]
    both = jnp.concatenate([pick_ew[...].astype(F32), pick], axis=0)
    place_out[...] = jnp.transpose(both).astype(BF16)
    weight = 1.0 / mult[...].astype(F32)
    weight_out[...] = as_columns(weight, NI)
    high, low = split(modes[...] * weight)
    modes_out[0] = high
    modes_out[1] = low
    edge_modes_out[0] = dot(high, place_out[...]).astype(BF16)
    edge_modes_out[1] = dot(low, place_out[...]).astype(BF16)
    pre_out[...] = product(high, low, parts)
    a, b = split(jnp.transpose(tile[...]))
    tile_out[0] = a
    tile_out[1] = b


def matrix_body(scaled, *refs):
    mat, pick_ew, pick_ns = refs[:3]
    full, edge, token = refs[-3:]
    token[...] = jnp.zeros_like(token)

    def halves(rows):
        value = mat[rows, :]
        if scaled:
            mult, column = refs[3:5]
            value = value * (1.0 / mult[...].astype(F32)) * column[rows, 0:1]
        a, b = split(value)
        full[0, rows, :] = a
        full[1, rows, :] = b

    by_rows(NI, 128, halves)

    def picked(level, carry):
        edge[level, :SIDE, :] = dot(pick_ew[...], full[level]).astype(BF16)
        edge[level, SIDE:, :] = dot(pick_ns[...], full[level]).astype(BF16)
        return carry

    lax.fori_loop(0, 2, picked, 0)


def corner_body(edge, place, out, token):
    token[...] = jnp.zeros_like(token)

    def level(i, carry):
        by_rows(NB, SIDE, lambda rows: step(i, rows))
        return carry

    def step(i, rows):
        out[i, rows, :] = dot(edge[i, rows, :], place[...]).astype(BF16)

    lax.fori_loop(0, 2, level, 0)


def close_body(sign, *refs):
    pre, edge_modes, edge_out, rhs_out = refs[-4:]
    edge = received(refs[:-4])
    edge_out[...] = edge
    t = product(edge_modes[0], edge_modes[1], split(edge))
    rhs = pre[...] + t if sign > 0 else pre[...] - t
    for i in range(rhs_out.shape[0]):
        rhs_out[i] = rhs


def rest_body(sign, base, edge, place, r_out, token, parts):
    token[...] = jnp.zeros_like(token)
    keep_halves(parts, edge)
    fill(r_out, base)
    add_select(r_out, place, parts, sign)


def final_body(*refs):
    mid, place, r_out, edge, parts = refs[-5:]
    edge[...] = received(refs[:-5])
    keep_halves(parts, edge)
    fill(r_out, mid)
    add_select(r_out, place, parts, -1)


def coarse_body(shares, tile, out):
    gathered = jnp.concatenate([shares[i] for i in range(shares.shape[0])], axis=0)
    parts = split(gathered)

    def step(rows):
        out[rows, :] = product(tile[0, rows, :], tile[1, rows, :], parts)

    by_rows(tile.shape[1], 256, step)


def spread_body(shares, edge_modes, sol_out, *packets):
    sol = jnp.sum(shares[...], axis=0)
    sol_out[...] = sol
    put_packets(product(edge_modes[0], edge_modes[1], split(sol), dot_t), *packets)


def spread_rest_body(sol, modes, c_out, token):
    token[...] = jnp.zeros_like(token)
    c_out[...] = product(modes[0], modes[1], split(sol[...]), dot_t)


def apply_body(sign, *refs):
    pre, corner, edge_out = refs[-7:-4]
    edge = received(refs[:-7])
    edge_out[...] = edge
    rows = SIDE + 2 * FACE
    t = product(corner[0, :rows, :], corner[1, :rows, :], split(edge))
    put_packets(pre[:rows, :] + t if sign > 0 else pre[:rows, :] - t, *refs[-4:])


def apply_rest_body(fresh, *refs):
    edge, local, r, place, full = refs[:5]
    mid_out, x_out, token, edge_parts, parts, v = refs[-6:]
    token[...] = jnp.zeros_like(token)
    keep_halves(edge_parts, edge)
    fill(v, local)
    add_select(v, place, edge_parts, 1)

    def step(rows):
        x_out[rows, :] = v[rows, :] if fresh else refs[5][rows, :] + v[rows, :]
        parts[0, rows, :], parts[1, rows, :] = split(v[rows, :])
        mid_out[rows, :] = r[rows, :]

    by_rows(NI, 128, step)
    add_product(mid_out, full, parts, -1)


def solve_rest_body(edge, mid, place, full, r_out, g_out, token, edge_parts, parts):
    token[...] = jnp.zeros_like(token)
    keep_halves(edge_parts, edge)
    fill(r_out, mid)
    add_select(r_out, place, edge_parts, -1)
    keep_halves(parts, r_out)
    fill(g_out, None)
    add_product(g_out, full, parts, 1)


def local_body(mat, v, out, parts):
    keep_halves(parts, v)
    fill(out, None)
    add_product(out, mat, parts, 1)


def on_device(rows, cols, local_load, schur, solver, modes, inverse, share_rows, share_count, mult):
    both = ("row", "col")

    def shifted(value, target):
        pairs = [(a * cols + b, target(a, b)) for a in range(rows) for b in range(cols)]
        return lax.ppermute(value, both, pairs)

    def partner_of(i, k, count):
        return (((i + k) ^ 1) - k) % count

    def by_col(value, k):
        return shifted(value, lambda a, b: a * cols + partner_of(b, k, cols))

    def by_row(value, k):
        return shifted(value, lambda a, b: partner_of(a, k, rows) * cols + b)

    def depart(side0, side1, face0, face1):
        return by_col(side0, 0), by_col(side1, 1), by_row(face0, 0), by_row(face1, 1)

    def turn(arrived, *tokens):
        corners = call(turn_body, [((2 * CORNER, RHS), F32)] * 2, arrived[:2], after=tokens)
        return *arrived, by_row(corners[0], 0), by_row(corners[1], 1)

    def local(mat, v):
        return call(local_body, [((mat.shape[1], RHS), F32)], (mat, v), scratch=[PARTS])[0]

    lists, counts = share_rows[0, 0], share_count[0, 0]
    load = local_load[0, 0]

    half_pick = ((SIDE, NI), BF16)
    pick_ew, *sides = call(start_body, [half_pick, *BUNDLES], (counts, lists, load), smem=1)
    pick_ns, place, weight, modes_s, edge_modes, tile, pre, *faces = call(
        start_rest_body,
        [
            half_pick,
            ((NI, NB), BF16),
            ((NI, 128), F32),
            ((2, MODES, NI), BF16),
            ((2, MODES, NB), BF16),
            ((2, 512, 256), BF16),
            BLOCK,
            *FACES,
        ],
        (counts, lists, pick_ew, mult[0], load, modes[0, 0], inverse[0, 0].reshape(256, 512)),
        smem=1,
    )
    arrived = depart(*sides, *faces)

    matrices = [((2, NI, NI), BF16), ((2, NB, NI), BF16), TOKEN]
    corner_shape = [((2, NB, NB), BF16), TOKEN]
    schur_full, schur_edge, schur_token = call(
        functools.partial(matrix_body, False), matrices, (schur[0, 0], pick_ew, pick_ns)
    )
    schur_corner, corner_token = call(corner_body, corner_shape, (schur_edge, place))

    arrived = turn(arrived, schur_token)

    copies = ((rows, MODES, RHS), F32)
    edge, rhs = call(
        functools.partial(close_body, 1), [EDGE, copies], (*arrived, pre, edge_modes), after=(corner_token,)
    )
    x = mid = None
    for step in range(STEPS):
        shares = lax.all_to_all(rhs, "row", 0, 0, tiled=True)
        (partial,) = call(
            coarse_body,
            [((cols * MODES, RHS), F32)],
            (shares, tile),
        )
        shares = lax.all_to_all(partial.reshape(cols, MODES, RHS), "col", 0, 0, tiled=True)
        sol, *packets = call(spread_body, [BLOCK, *PACKETS], (shares, edge_modes))
        arrived = depart(*packets)
        c, token = call(spread_rest_body, [FULL, TOKEN], (sol, modes_s))
        sign, base = (1, load) if step == 0 else (-1, mid)
        r, r_token = call(
            functools.partial(rest_body, sign),
            [FULL, TOKEN],
            (base, edge, place),
            scratch=[EDGE_PARTS],
            after=(token,),
        )
        if step == 0:
            solver_full, solver_edge, solver_token = call(
                functools.partial(matrix_body, True),
                matrices,
                (solver[0, 0], pick_ew, pick_ns, mult[0], weight),
                after=(sol,),
            )
            solver_corner, corner_token = call(corner_body, corner_shape, (solver_edge, place))
            arrived = turn(arrived, r_token, solver_token)
        else:
            arrived = turn(arrived, r_token)
        pre = local(schur_edge, c)

        def apply(arrived, pre, v, r, x):
            edge, *packets = call(
                functools.partial(apply_body, 1), [EDGE, *PACKETS], (*arrived, pre, schur_corner)
            )
            arrived = depart(*packets)
            fresh = x is None
            args = [edge, v, r, place, schur_full] + ([] if fresh else [x])
            mid, x, token = call(functools.partial(apply_rest_body, fresh), [FULL, FULL, TOKEN], args, scratch=[EDGE_PARTS, PARTS, pltpu.VMEM((NI, RHS), F32)])
            return turn(arrived, token), mid, x

        arrived, mid, x = apply(arrived, pre, c, r, x)
        pre = local(solver_edge, mid)

        edge, *packets = call(functools.partial(apply_body, -1), [EDGE, *PACKETS], (*arrived, pre, solver_corner))
        arrived = depart(*packets)
        r, g, token = call(
            solve_rest_body, [FULL, FULL, TOKEN], (edge, mid, place, solver_full), scratch=[EDGE_PARTS, PARTS]
        )
        arrived = turn(arrived, token)
        pre = local(schur_edge, g)

        last = step == STEPS - 1
        arrived, mid, x = apply(arrived, pre, g, r, x)
        if last:
            (residual,) = call(final_body, [FULL], (*arrived, mid, place), scratch=EDGE_SCRATCH)
        else:
            pre = local(modes_s, mid)
            edge, rhs = call(functools.partial(close_body, -1), [EDGE, copies], (*arrived, pre, edge_modes))
    return x[None, None], residual[None, None]


def solution(mesh):
    grid = P("row", "col")
    rows, cols = mesh.shape["row"], mesh.shape["col"]
    return jax.shard_map(
        functools.partial(on_device, rows, cols),
        mesh=mesh,
        in_specs=(grid,) * 8,
        out_specs=(grid, grid),
        check_vma=False,
    )
```

```python
import functools

import jax
import jax.numpy as jnp
from jax import lax
from jax.experimental import pallas as pl
from jax.experimental.pallas import tpu as pltpu
from jax.sharding import PartitionSpec as P

NI = 1024
RHS = 256
MODES = 32
FACE = 128
CORNER = 16
STEPS = 2
BUNDLE = FACE + 2 * CORNER
SIDE = 2 * BUNDLE
SLOTS = SIDE + 2 * FACE
NB = 2 * SIDE
F32 = jnp.float32
BF16 = jnp.bfloat16


def dot(a, b):
    return jnp.dot(a, b, preferred_element_type=F32)


def dot_t(a, b):
    return lax.dot_general(a, b, (((0,), (0,)), ((), ())), preferred_element_type=F32)


def split(v):
    high = v.astype(BF16)
    return high, (v - high.astype(F32)).astype(BF16)


def product(mat_high, mat_low, parts, mul=dot):
    high, low = parts
    return mul(mat_high, high) + mul(mat_high, low) + mul(mat_low, high)


def select(onehot, parts):
    high, low = parts
    return dot(onehot, high) + dot(onehot, low)


def keep_halves(parts, v):
    def step(rows):
        parts[0, rows, :], parts[1, rows, :] = split(v[rows, :])

    by_rows(v.shape[0], min(v.shape[0], 128), step)


def by_rows(count, size, step):
    def once(i, carry):
        step(pl.ds(pl.multiple_of(i * size, size), size))
        return carry

    lax.fori_loop(0, count // size, once, 0)


def call(body, out_shapes, args, scratch=(), smem=0, after=(), limit=6):
    count = len(args)

    def run(*refs):
        return body(*refs[:count], *refs[count + len(after) :])

    specs = [pl.BlockSpec(memory_space=pltpu.SMEM)] * smem
    specs += [pl.BlockSpec(memory_space=pltpu.VMEM)] * (count - smem)
    specs += [pl.BlockSpec(memory_space=pltpu.VMEM)] * len(after)
    return pl.pallas_call(
        run,
        name=getattr(body, "func", body).__name__,
        out_shape=[jax.ShapeDtypeStruct(s, d) for s, d in out_shapes],
        in_specs=specs,
        out_specs=[pl.BlockSpec(memory_space=pltpu.VMEM)] * len(out_shapes),
        scratch_shapes=list(scratch),
        compiler_params=pltpu.CompilerParams(vmem_limit_bytes=limit << 20),
    )(*args, *after)


PARTS = pltpu.VMEM((2, NI, RHS), BF16)
HALVES = [pltpu.VMEM((NI, RHS), BF16)] * 2
BLK = 256
FULL = ((NI, RHS), F32)
EDGE = ((NB, RHS), F32)
BLOCK = ((MODES, RHS), F32)
TOKEN = ((8, 128), F32)
FACES = [((FACE, RHS), F32)] * 2
BUNDLES = [((BUNDLE, RHS), F32)] * 2
PACKETS = BUNDLES + FACES


def put_packets(v, side0, side1, face0, face1):
    side0[...] = v[:BUNDLE]
    side1[...] = v[BUNDLE:SIDE]
    face0[...] = v[SIDE : SIDE + FACE]
    face1[...] = v[SIDE + FACE : SIDE + 2 * FACE]


def received(arrivals):
    side0, side1, face0, face1, corner0, corner1 = (ref[...] for ref in arrivals)
    end = CORNER + FACE
    return jnp.concatenate(
        [
            corner0[:CORNER],
            side0[CORNER:end],
            corner1[:CORNER],
            corner0[CORNER:],
            side1[CORNER:end],
            corner1[CORNER:],
            face0,
            face1,
            jnp.zeros((NB - SIDE - 2 * FACE, RHS), F32),
        ],
        axis=0,
    )


def turn_body(side0, side1, corner0, corner1):
    end = CORNER + FACE
    corner0[...] = jnp.concatenate([side0[:CORNER], side1[:CORNER]], axis=0)
    corner1[...] = jnp.concatenate([side0[end:], side1[end:]], axis=0)


def as_columns(row, width):
    return jnp.transpose(jnp.broadcast_to(row, (128, width)))


def slot_keys(lists, counts):
    turn_row, turn_col = lax.rem(lax.axis_index("row"), 2), lax.rem(lax.axis_index("col"), 2)
    blocks = []
    for p, q, size in SLOT_LISTS:
        a = p if p == 1 else p + 2 * (1 - p) * turn_row
        b = q if q == 1 else q + 2 * (1 - q) * turn_col
        ids = lax.broadcasted_iota(jnp.int32, (1, FACE), 1)
        row = jnp.where(ids < counts[a, b], lists[a, pl.ds(b, 1), :], -1).astype(F32)
        blocks.append(as_columns(row, FACE)[:size])
    return jnp.concatenate(blocks, axis=0)


SLOT_LISTS = (
    (2, 2, CORNER),
    (1, 2, FACE),
    (0, 2, CORNER),
    (2, 0, CORNER),
    (1, 0, FACE),
    (0, 0, CORNER),
    (2, 1, FACE),
    (0, 1, FACE),
)


def start_body(counts, lists, load, pick_out, *packets):
    keys = slot_keys(lists, counts)[:, 0:1]
    lanes = lax.broadcasted_iota(jnp.int32, (SLOTS, NI), 1).astype(F32)
    pick = jnp.where(keys == lanes, 1.0, 0.0).astype(BF16)
    pick_out[:SLOTS, :] = pick
    pick_out[SLOTS:, :] = jnp.zeros((NB - SLOTS, NI), BF16)
    put_packets(select(pick, split(load[...])), *packets)


def start_rest_body(pick, mult, load, modes, tile, place_out, weight_out, modes_out, edge_modes_out, tile_out, pre_out):
    def turned(cols):
        place_out[cols, :] = jnp.transpose(pick[:, cols].astype(F32)).astype(BF16)

    for blk in range(4):
        turned(slice(256 * blk, 256 * (blk + 1)))
    weight = 1.0 / mult[...].astype(F32)
    weight_out[...] = as_columns(weight, NI)
    high, low = split(modes[...] * weight)
    modes_out[0] = high
    modes_out[1] = low
    edge_modes_out[0] = dot(high, place_out[...]).astype(BF16)
    edge_modes_out[1] = dot(low, place_out[...]).astype(BF16)
    pre_out[...] = product(high, low, split(load[...]))
    a, b = split(jnp.transpose(tile[...]))
    tile_out[0] = a
    tile_out[1] = b


def matrix_body(scaled, *refs):
    mat, pick = refs[:2]
    full, edge, token = refs[-3:]
    token[...] = jnp.zeros_like(token)

    def halves(rows):
        value = mat[rows, :]
        if scaled:
            mult, column = refs[2:4]
            value = value * (1.0 / mult[...].astype(F32)) * column[rows, 0:1]
        a, b = split(value)
        full[0, rows, :] = a
        full[1, rows, :] = b

    by_rows(NI, 128, halves)

    def picked(i, carry):
        rows = pl.ds(pl.multiple_of(lax.rem(i, 2) * SIDE, SIDE), SIDE)
        edge[lax.div(i, 2), rows, :] = dot(pick[rows, :], full[lax.div(i, 2)]).astype(BF16)
        return carry

    lax.fori_loop(0, 4, picked, 0)


def corner_body(edge, place, out, token):
    token[...] = jnp.zeros_like(token)

    def level(i, carry):
        by_rows(NB, SIDE, lambda rows: step(i, rows))
        return carry

    def step(i, rows):
        out[i, rows, :] = dot(edge[i, rows, :], place[...]).astype(BF16)

    lax.fori_loop(0, 2, level, 0)


def close_body(sign, *refs):
    pre, edge_modes, edge_out, rhs_out = refs[-4:]
    edge = received(refs[:-4])
    edge_out[...] = edge
    t = product(edge_modes[0], edge_modes[1], split(edge))
    rhs = pre[...] + t if sign > 0 else pre[...] - t
    for i in range(rhs_out.shape[0]):
        rhs_out[i] = rhs


def rest_body(sign, base, edge, place, r_out, token):
    token[...] = jnp.zeros_like(token)
    parts = split(edge[...])

    def step(rows):
        arrived = select(place[rows, :], parts)
        r_out[rows, :] = base[rows, :] + arrived if sign > 0 else base[rows, :] - arrived

    by_rows(NI, BLK, step)


def final_body(*refs):
    mid, place, r_out = refs[-3:]
    parts = split(received(refs[:-3]))

    def step(rows):
        r_out[rows, :] = mid[rows, :] - select(place[rows, :], parts)

    by_rows(NI, BLK, step)


def coarse_body(shares, tile, out):
    gathered = jnp.concatenate([shares[i] for i in range(shares.shape[0])], axis=0)
    parts = split(gathered)

    def step(rows):
        out[rows, :] = product(tile[0, rows, :], tile[1, rows, :], parts)

    by_rows(tile.shape[1], 256, step)


def spread_body(shares, edge_modes, sol_out, *packets):
    sol = jnp.sum(shares[...], axis=0)
    sol_out[...] = sol
    put_packets(product(edge_modes[0], edge_modes[1], split(sol), dot_t), *packets)


def spread_rest_body(sol, modes, c_out, token):
    token[...] = jnp.zeros_like(token)
    parts = split(sol[...])

    def step(rows):
        c_out[rows, :] = product(modes[0, :, rows], modes[1, :, rows], parts, dot_t)

    by_rows(NI, BLK, step)


def apply_body(sign, *refs):
    pre, corner, edge_out = refs[-7:-4]
    edge = received(refs[:-7])
    edge_out[...] = edge
    rows = SIDE + 2 * FACE
    t = product(corner[0, :rows, :], corner[1, :rows, :], split(edge))
    put_packets(pre[:rows, :] + t if sign > 0 else pre[:rows, :] - t, *refs[-4:])


def apply_rest_body(fresh, *refs):
    edge, local, r, place, full = refs[:5]
    mid_out, x_out, token, high, low = refs[-5:]
    token[...] = jnp.zeros_like(token)
    parts = split(edge[...])

    def vector(rows):
        v = local[rows, :] + select(place[rows, :], parts)
        x_out[rows, :] = v if fresh else refs[5][rows, :] + v
        high[rows, :], low[rows, :] = split(v)

    by_rows(NI, BLK, vector)

    def applied(rows):
        mid_out[rows, :] = r[rows, :] - product(full[0, rows, :], full[1, rows, :], (high[...], low[...]))

    by_rows(NI, BLK, applied)


def solve_rest_body(edge, mid, place, full, r_out, g_out, token, high, low):
    token[...] = jnp.zeros_like(token)
    parts = split(edge[...])

    def vector(rows):
        r = mid[rows, :] - select(place[rows, :], parts)
        r_out[rows, :] = r
        high[rows, :], low[rows, :] = split(r)

    by_rows(NI, BLK, vector)

    def applied(rows):
        g_out[rows, :] = product(full[0, rows, :], full[1, rows, :], (high[...], low[...]))

    by_rows(NI, BLK, applied)


def local_body(mat, v, out, parts):
    keep_halves(parts, v)
    count = mat.shape[1]

    def step(rows):
        out[rows, :] = product(mat[0, rows, :], mat[1, rows, :], (parts[0], parts[1]))

    by_rows(count, min(count, SIDE), step)


def on_device(rows, cols, local_load, schur, solver, modes, inverse, share_rows, share_count, mult):
    both = ("row", "col")

    def shifted(value, target):
        pairs = [(a * cols + b, target(a, b)) for a in range(rows) for b in range(cols)]
        return lax.ppermute(value, both, pairs)

    def partner_of(i, k, count):
        return (((i + k) ^ 1) - k) % count

    def by_col(value, k):
        return shifted(value, lambda a, b: a * cols + partner_of(b, k, cols))

    def by_row(value, k):
        return shifted(value, lambda a, b: partner_of(a, k, rows) * cols + b)

    def depart(side0, side1, face0, face1):
        return by_col(side0, 0), by_col(side1, 1), by_row(face0, 0), by_row(face1, 1)

    def turn(arrived, *tokens):
        corners = call(turn_body, [((2 * CORNER, RHS), F32)] * 2, arrived[:2], after=tokens)
        return *arrived, by_row(corners[0], 0), by_row(corners[1], 1)

    def local(mat, v):
        return call(local_body, [((mat.shape[1], RHS), F32)], (mat, v), scratch=[PARTS])[0]

    lists, counts = share_rows[0, 0], share_count[0, 0]
    load = local_load[0, 0]

    pick, *packets = call(start_body, [((NB, NI), BF16), *PACKETS], (counts, lists, load), smem=1)
    arrived = depart(*packets)
    place, weight, modes_s, edge_modes, tile, pre = call(
        start_rest_body,
        [
            ((NI, NB), BF16),
            ((NI, 128), F32),
            ((2, MODES, NI), BF16),
            ((2, MODES, NB), BF16),
            ((2, 512, 256), BF16),
            BLOCK,
        ],
        (pick, mult[0], load, modes[0, 0], inverse[0, 0].reshape(256, 512)),
    )

    matrices = [((2, NI, NI), BF16), ((2, NB, NI), BF16), TOKEN]
    corner_shape = [((2, NB, NB), BF16), TOKEN]
    schur_full, schur_edge, schur_token = call(
        functools.partial(matrix_body, False), matrices, (schur[0, 0], pick)
    )
    schur_corner, corner_token = call(corner_body, corner_shape, (schur_edge, place))

    arrived = turn(arrived, schur_token)

    copies = ((rows, MODES, RHS), F32)
    edge, rhs = call(
        functools.partial(close_body, 1), [EDGE, copies], (*arrived, pre, edge_modes), after=(corner_token,)
    )
    x = mid = None
    for step in range(STEPS):
        shares = lax.all_to_all(rhs, "row", 0, 0, tiled=True)
        (partial,) = call(
            coarse_body,
            [((cols * MODES, RHS), F32)],
            (shares, tile),
        )
        shares = lax.all_to_all(partial.reshape(cols, MODES, RHS), "col", 0, 0, tiled=True)
        sol, *packets = call(spread_body, [BLOCK, *PACKETS], (shares, edge_modes))
        arrived = depart(*packets)
        c, token = call(spread_rest_body, [FULL, TOKEN], (sol, modes_s))
        sign, base = (1, load) if step == 0 else (-1, mid)
        r, r_token = call(
            functools.partial(rest_body, sign),
            [FULL, TOKEN],
            (base, edge, place),
            after=(token,),
        )
        if step == 0:
            solver_full, solver_edge, solver_token = call(
                functools.partial(matrix_body, True),
                matrices,
                (solver[0, 0], pick, mult[0], weight),
                after=(sol,),
            )
            solver_corner, corner_token = call(corner_body, corner_shape, (solver_edge, place))
            arrived = turn(arrived, r_token, solver_token)
        else:
            arrived = turn(arrived, r_token)
        pre = local(schur_edge, c)

        def apply(arrived, pre, v, r, x):
            edge, *packets = call(
                functools.partial(apply_body, 1), [EDGE, *PACKETS], (*arrived, pre, schur_corner)
            )
            arrived = depart(*packets)
            fresh = x is None
            args = [edge, v, r, place, schur_full] + ([] if fresh else [x])
            mid, x, token = call(functools.partial(apply_rest_body, fresh), [FULL, FULL, TOKEN], args, scratch=HALVES)
            return turn(arrived, token), mid, x

        arrived, mid, x = apply(arrived, pre, c, r, x)
        pre = local(solver_edge, mid)

        edge, *packets = call(functools.partial(apply_body, -1), [EDGE, *PACKETS], (*arrived, pre, solver_corner))
        arrived = depart(*packets)
        r, g, token = call(
            solve_rest_body, [FULL, FULL, TOKEN], (edge, mid, place, solver_full), scratch=HALVES
        )
        arrived = turn(arrived, token)
        pre = local(schur_edge, g)

        last = step == STEPS - 1
        arrived, mid, x = apply(arrived, pre, g, r, x)
        if last:
            (residual,) = call(final_body, [FULL], (*arrived, mid, place))
        else:
            pre = local(modes_s, mid)
            edge, rhs = call(functools.partial(close_body, -1), [EDGE, copies], (*arrived, pre, edge_modes))
    return x[None, None], residual[None, None]


def solution(mesh):
    grid = P("row", "col")
    rows, cols = mesh.shape["row"], mesh.shape["col"]
    return jax.shard_map(
        functools.partial(on_device, rows, cols),
        mesh=mesh,
        in_specs=(grid,) * 8,
        out_specs=(grid, grid),
        check_vma=False,
    )
```

```python
import functools

import jax
import jax.numpy as jnp
from jax import lax
from jax.experimental import pallas as pl
from jax.experimental.pallas import tpu as pltpu
from jax.sharding import PartitionSpec as P

NI = 1024
RHS = 256
MODES = 32
FACE = 128
CORNER = 16
STEPS = 2
BUNDLE = FACE + 2 * CORNER
SIDE = 2 * BUNDLE
SLOTS = SIDE + 2 * FACE
NB = 2 * SIDE
F32 = jnp.float32
BF16 = jnp.bfloat16


def dot(a, b):
    return jnp.dot(a, b, preferred_element_type=F32)


def dot_t(a, b):
    return lax.dot_general(a, b, (((0,), (0,)), ((), ())), preferred_element_type=F32)


def split(v):
    high = v.astype(BF16)
    return high, (v - high.astype(F32)).astype(BF16)


def product(mat_high, mat_low, parts, mul=dot):
    high, low = parts
    return mul(mat_high, high) + mul(mat_high, low) + mul(mat_low, high)


def select(onehot, parts):
    high, low = parts
    return dot(onehot, high) + dot(onehot, low)


def keep_halves(parts, v):
    def step(rows):
        parts[0, rows, :], parts[1, rows, :] = split(v[rows, :])

    by_rows(v.shape[0], min(v.shape[0], 128), step)


def by_rows(count, size, step):
    def once(i, carry):
        step(pl.ds(pl.multiple_of(i * size, size), size))
        return carry

    lax.fori_loop(0, count // size, once, 0)


def call(body, out_shapes, args, scratch=(), smem=0, after=(), limit=6):
    count = len(args)

    def run(*refs):
        return body(*refs[:count], *refs[count + len(after) :])

    specs = [pl.BlockSpec(memory_space=pltpu.SMEM)] * smem
    specs += [pl.BlockSpec(memory_space=pltpu.VMEM)] * (count - smem)
    specs += [pl.BlockSpec(memory_space=pltpu.VMEM)] * len(after)
    return pl.pallas_call(
        run,
        name=getattr(body, "func", body).__name__,
        out_shape=[jax.ShapeDtypeStruct(s, d) for s, d in out_shapes],
        in_specs=specs,
        out_specs=[pl.BlockSpec(memory_space=pltpu.VMEM)] * len(out_shapes),
        scratch_shapes=list(scratch),
        compiler_params=pltpu.CompilerParams(vmem_limit_bytes=limit << 20),
    )(*args, *after)


PARTS = pltpu.VMEM((2, NI, RHS), BF16)
HALVES = [pltpu.VMEM((NI, RHS), BF16)] * 2
BLK = 256
FULL = ((NI, RHS), F32)
EDGE = ((NB, RHS), F32)
BLOCK = ((MODES, RHS), F32)
TOKEN = ((8, 128), F32)
FACES = [((FACE, RHS), F32)] * 2
BUNDLES = [((BUNDLE, RHS), F32)] * 2
PACKETS = BUNDLES + FACES


def put_packets(v, side0, side1, face0, face1):
    side0[...] = v[:BUNDLE]
    side1[...] = v[BUNDLE:SIDE]
    face0[...] = v[SIDE : SIDE + FACE]
    face1[...] = v[SIDE + FACE : SIDE + 2 * FACE]


def received(arrivals):
    side0, side1, face0, face1, corner0, corner1 = (ref[...] for ref in arrivals)
    end = CORNER + FACE
    return jnp.concatenate(
        [
            corner0[:CORNER],
            side0[CORNER:end],
            corner1[:CORNER],
            corner0[CORNER:],
            side1[CORNER:end],
            corner1[CORNER:],
            face0,
            face1,
            jnp.zeros((NB - SIDE - 2 * FACE, RHS), F32),
        ],
        axis=0,
    )


def turn_body(side0, side1, corner0, corner1):
    end = CORNER + FACE
    corner0[...] = jnp.concatenate([side0[:CORNER], side1[:CORNER]], axis=0)
    corner1[...] = jnp.concatenate([side0[end:], side1[end:]], axis=0)


def as_columns(row, width):
    return jnp.transpose(jnp.broadcast_to(row, (128, width)))


def slot_keys(lists, counts):
    turn_row, turn_col = lax.rem(lax.axis_index("row"), 2), lax.rem(lax.axis_index("col"), 2)
    blocks = []
    for p, q, size in SLOT_LISTS:
        a = p if p == 1 else p + 2 * (1 - p) * turn_row
        b = q if q == 1 else q + 2 * (1 - q) * turn_col
        ids = lax.broadcasted_iota(jnp.int32, (1, FACE), 1)
        row = jnp.where(ids < counts[a, b], lists[a, pl.ds(b, 1), :], -1).astype(F32)
        blocks.append(as_columns(row, FACE)[:size])
    return jnp.concatenate(blocks, axis=0)


SLOT_LISTS = (
    (2, 2, CORNER),
    (1, 2, FACE),
    (0, 2, CORNER),
    (2, 0, CORNER),
    (1, 0, FACE),
    (0, 0, CORNER),
    (2, 1, FACE),
    (0, 1, FACE),
)


def start_body(counts, lists, load, pick_out, *packets):
    keys = slot_keys(lists, counts)[:, 0:1]
    lanes = lax.broadcasted_iota(jnp.int32, (SLOTS, NI), 1).astype(F32)
    pick = jnp.where(keys == lanes, 1.0, 0.0).astype(BF16)
    pick_out[:SLOTS, :] = pick
    pick_out[SLOTS:, :] = jnp.zeros((NB - SLOTS, NI), BF16)
    put_packets(select(pick, split(load[...])), *packets)


def start_rest_body(pick, mult, load, modes, tile, place_out, weight_out, modes_out, edge_modes_out, tile_out, pre_out):
    def turned(cols):
        place_out[cols, :] = jnp.transpose(pick[:, cols].astype(F32)).astype(BF16)

    for blk in range(4):
        turned(slice(256 * blk, 256 * (blk + 1)))
    weight = 1.0 / mult[...].astype(F32)
    weight_out[...] = as_columns(weight, NI)
    high, low = split(modes[...] * weight)
    modes_out[0] = high
    modes_out[1] = low
    edge_modes_out[0] = dot(high, place_out[...]).astype(BF16)
    edge_modes_out[1] = dot(low, place_out[...]).astype(BF16)
    pre_out[...] = product(high, low, split(load[...]))
    a, b = split(jnp.transpose(tile[...]))
    tile_out[0] = a
    tile_out[1] = b


def matrix_body(scaled, *refs):
    mat, pick = refs[:2]
    full, edge, token = refs[-3:]
    token[...] = jnp.zeros_like(token)

    def halves(rows):
        value = mat[rows, :]
        if scaled:
            mult, column = refs[2:4]
            value = value * (1.0 / mult[...].astype(F32)) * column[rows, 0:1]
        a, b = split(value)
        full[0, rows, :] = a
        full[1, rows, :] = b

    by_rows(NI, 128, halves)

    def picked(i, carry):
        rows = pl.ds(pl.multiple_of(lax.rem(i, 2) * SIDE, SIDE), SIDE)
        edge[lax.div(i, 2), rows, :] = dot(pick[rows, :], full[lax.div(i, 2)]).astype(BF16)
        return carry

    lax.fori_loop(0, 4, picked, 0)


def corner_body(edge, place, out, token):
    token[...] = jnp.zeros_like(token)

    def level(i, carry):
        by_rows(NB, SIDE, lambda rows: step(i, rows))
        return carry

    def step(i, rows):
        out[i, rows, :] = dot(edge[i, rows, :], place[...]).astype(BF16)

    lax.fori_loop(0, 2, level, 0)


def close_body(sign, *refs):
    pre, edge_modes, edge_out, rhs_out = refs[-4:]
    edge = received(refs[:-4])
    edge_out[...] = edge
    t = product(edge_modes[0], edge_modes[1], split(edge))
    rhs = pre[...] + t if sign > 0 else pre[...] - t
    for i in range(rhs_out.shape[0]):
        rhs_out[i] = rhs


def rest_body(sign, base, edge, place, r_out, token):
    token[...] = jnp.zeros_like(token)
    parts = split(edge[...])

    def step(rows):
        arrived = select(place[rows, :], parts)
        r_out[rows, :] = base[rows, :] + arrived if sign > 0 else base[rows, :] - arrived

    by_rows(NI, BLK, step)


def final_body(*refs):
    mid, place, r_out = refs[-3:]
    parts = split(received(refs[:-3]))

    def step(rows):
        r_out[rows, :] = mid[rows, :] - select(place[rows, :], parts)

    by_rows(NI, BLK, step)


def coarse_body(shares, tile, out):
    gathered = jnp.concatenate([shares[i] for i in range(shares.shape[0])], axis=0)
    parts = split(gathered)

    def step(rows):
        out[rows, :] = product(tile[0, rows, :], tile[1, rows, :], parts)

    by_rows(tile.shape[1], 256, step)


def spread_body(shares, edge_modes, sol_out, *packets):
    sol = jnp.sum(shares[...], axis=0)
    sol_out[...] = sol
    put_packets(product(edge_modes[0], edge_modes[1], split(sol), dot_t), *packets)


def spread_rest_body(sol, modes, c_out, token):
    token[...] = jnp.zeros_like(token)
    parts = split(sol[...])

    def step(rows):
        c_out[rows, :] = product(modes[0, :, rows], modes[1, :, rows], parts, dot_t)

    by_rows(NI, BLK, step)


def apply_body(sign, *refs):
    pre, corner, edge_out = refs[-7:-4]
    edge = received(refs[:-7])
    edge_out[...] = edge
    rows = SIDE + 2 * FACE
    t = product(corner[0, :rows, :], corner[1, :rows, :], split(edge))
    put_packets(pre[:rows, :] + t if sign > 0 else pre[:rows, :] - t, *refs[-4:])


def apply_rest_body(fresh, *refs):
    edge, local, r, place, full = refs[:5]
    mid_out, x_out, token, high, low = refs[-5:]
    token[...] = jnp.zeros_like(token)
    parts = split(edge[...])

    def vector(rows):
        v = local[rows, :] + select(place[rows, :], parts)
        x_out[rows, :] = v if fresh else refs[5][rows, :] + v
        high[rows, :], low[rows, :] = split(v)

    by_rows(NI, BLK, vector)

    def applied(rows):
        mid_out[rows, :] = r[rows, :] - product(full[0, rows, :], full[1, rows, :], (high[...], low[...]))

    by_rows(NI, BLK, applied)


def solve_rest_body(edge, mid, place, full, r_out, g_out, token, high, low):
    token[...] = jnp.zeros_like(token)
    parts = split(edge[...])

    def vector(rows):
        r = mid[rows, :] - select(place[rows, :], parts)
        r_out[rows, :] = r
        high[rows, :], low[rows, :] = split(r)

    by_rows(NI, BLK, vector)

    def applied(rows):
        g_out[rows, :] = product(full[0, rows, :], full[1, rows, :], (high[...], low[...]))

    by_rows(NI, BLK, applied)


def local_body(mat, v, out, parts):
    keep_halves(parts, v)
    count = mat.shape[1]

    def step(rows):
        out[rows, :] = product(mat[0, rows, :], mat[1, rows, :], (parts[0], parts[1]))

    by_rows(count, min(count, SIDE), step)


def on_device(rows, cols, local_load, schur, solver, modes, inverse, share_rows, share_count, mult):
    both = ("row", "col")

    def shifted(value, target):
        pairs = [(a * cols + b, target(a, b)) for a in range(rows) for b in range(cols)]
        return lax.ppermute(value, both, pairs)

    def partner_of(i, k):
        return ((i + k) ^ 1) - k

    def by_col(value, k):
        def target(a, b):
            other = partner_of(b, k)
            return a * cols + other if 0 <= other < cols else (a ^ 1) * cols + b

        return shifted(value, target)

    def by_row(value, k):
        def target(a, b):
            other = partner_of(a, k)
            return other * cols + b if 0 <= other < rows else a * cols + (b ^ 4)

        return shifted(value, target)

    def depart(side0, side1, face0, face1):
        return by_col(side0, 0), by_col(side1, 1), by_row(face0, 0), by_row(face1, 1)

    def turn(arrived, *tokens):
        corners = call(turn_body, [((2 * CORNER, RHS), F32)] * 2, arrived[:2], after=tokens)
        return *arrived, by_row(corners[0], 0), by_row(corners[1], 1)

    def local(mat, v):
        return call(local_body, [((mat.shape[1], RHS), F32)], (mat, v), scratch=[PARTS])[0]

    lists, counts = share_rows[0, 0], share_count[0, 0]
    load = local_load[0, 0]

    pick, *packets = call(start_body, [((NB, NI), BF16), *PACKETS], (counts, lists, load), smem=1)
    arrived = depart(*packets)
    place, weight, modes_s, edge_modes, tile, pre = call(
        start_rest_body,
        [
            ((NI, NB), BF16),
            ((NI, 128), F32),
            ((2, MODES, NI), BF16),
            ((2, MODES, NB), BF16),
            ((2, 512, 256), BF16),
            BLOCK,
        ],
        (pick, mult[0], load, modes[0, 0], inverse[0, 0].reshape(256, 512)),
    )

    matrices = [((2, NI, NI), BF16), ((2, NB, NI), BF16), TOKEN]
    corner_shape = [((2, NB, NB), BF16), TOKEN]
    schur_full, schur_edge, schur_token = call(
        functools.partial(matrix_body, False), matrices, (schur[0, 0], pick)
    )
    schur_corner, corner_token = call(corner_body, corner_shape, (schur_edge, place))

    arrived = turn(arrived, schur_token)

    copies = ((rows, MODES, RHS), F32)
    edge, rhs = call(
        functools.partial(close_body, 1), [EDGE, copies], (*arrived, pre, edge_modes), after=(corner_token,)
    )
    x = mid = None
    for step in range(STEPS):
        shares = lax.all_to_all(rhs, "row", 0, 0, tiled=True)
        (partial,) = call(
            coarse_body,
            [((cols * MODES, RHS), F32)],
            (shares, tile),
        )
        shares = lax.all_to_all(partial.reshape(cols, MODES, RHS), "col", 0, 0, tiled=True)
        sol, *packets = call(spread_body, [BLOCK, *PACKETS], (shares, edge_modes))
        arrived = depart(*packets)
        c, token = call(spread_rest_body, [FULL, TOKEN], (sol, modes_s))
        sign, base = (1, load) if step == 0 else (-1, mid)
        r, r_token = call(
            functools.partial(rest_body, sign),
            [FULL, TOKEN],
            (base, edge, place),
            after=(token,),
        )
        if step == 0:
            solver_full, solver_edge, solver_token = call(
                functools.partial(matrix_body, True),
                matrices,
                (solver[0, 0], pick, mult[0], weight),
                after=(sol,),
            )
            solver_corner, corner_token = call(corner_body, corner_shape, (solver_edge, place))
            arrived = turn(arrived, r_token, solver_token)
        else:
            arrived = turn(arrived, r_token)
        pre = local(schur_edge, c)

        def apply(arrived, pre, v, r, x):
            edge, *packets = call(
                functools.partial(apply_body, 1), [EDGE, *PACKETS], (*arrived, pre, schur_corner)
            )
            arrived = depart(*packets)
            fresh = x is None
            args = [edge, v, r, place, schur_full] + ([] if fresh else [x])
            mid, x, token = call(functools.partial(apply_rest_body, fresh), [FULL, FULL, TOKEN], args, scratch=HALVES)
            return turn(arrived, token), mid, x

        arrived, mid, x = apply(arrived, pre, c, r, x)
        pre = local(solver_edge, mid)

        edge, *packets = call(functools.partial(apply_body, -1), [EDGE, *PACKETS], (*arrived, pre, solver_corner))
        arrived = depart(*packets)
        r, g, token = call(
            solve_rest_body, [FULL, FULL, TOKEN], (edge, mid, place, solver_full), scratch=HALVES
        )
        arrived = turn(arrived, token)
        pre = local(schur_edge, g)

        last = step == STEPS - 1
        arrived, mid, x = apply(arrived, pre, g, r, x)
        if last:
            (residual,) = call(final_body, [FULL], (*arrived, mid, place))
        else:
            pre = local(modes_s, mid)
            edge, rhs = call(functools.partial(close_body, -1), [EDGE, copies], (*arrived, pre, edge_modes))
    return x[None, None], residual[None, None]


def solution(mesh):
    grid = P("row", "col")
    rows, cols = mesh.shape["row"], mesh.shape["col"]
    return jax.shard_map(
        functools.partial(on_device, rows, cols),
        mesh=mesh,
        in_specs=(grid,) * 8,
        out_specs=(grid, grid),
        check_vma=False,
    )
```

```python
import functools

import jax
import jax.numpy as jnp
from jax import lax
from jax.experimental import pallas as pl
from jax.experimental.pallas import tpu as pltpu
from jax.sharding import PartitionSpec as P

NI = 1024
RHS = 256
MODES = 32
FACE = 128
CORNER = 16
STEPS = 2
BUNDLE = FACE + 2 * CORNER
SIDE = 2 * BUNDLE
SLOTS = SIDE + 2 * FACE
NB = 2 * SIDE
F32 = jnp.float32
BF16 = jnp.bfloat16


def dot(a, b):
    return jnp.dot(a, b, preferred_element_type=F32)


def dot_t(a, b):
    return lax.dot_general(a, b, (((0,), (0,)), ((), ())), preferred_element_type=F32)


def split(v):
    high = v.astype(BF16)
    return high, (v - high.astype(F32)).astype(BF16)


def product(mat_high, mat_low, parts, mul=dot):
    high, low = parts
    return mul(mat_high, high) + mul(mat_high, low) + mul(mat_low, high)


def select(onehot, parts):
    high, low = parts
    return dot(onehot, high) + dot(onehot, low)


def keep_halves(parts, v):
    def step(rows):
        parts[0, rows, :], parts[1, rows, :] = split(v[rows, :])

    by_rows(v.shape[0], min(v.shape[0], 128), step)


def by_rows(count, size, step):
    def once(i, carry):
        step(pl.ds(pl.multiple_of(i * size, size), size))
        return carry

    lax.fori_loop(0, count // size, once, 0)


def call(body, out_shapes, args, scratch=(), smem=0, after=(), limit=6):
    count = len(args)

    def run(*refs):
        return body(*refs[:count], *refs[count + len(after) :])

    specs = [pl.BlockSpec(memory_space=pltpu.SMEM)] * smem
    specs += [pl.BlockSpec(memory_space=pltpu.VMEM)] * (count - smem)
    specs += [pl.BlockSpec(memory_space=pltpu.VMEM)] * len(after)
    return pl.pallas_call(
        run,
        name=getattr(body, "func", body).__name__,
        out_shape=[jax.ShapeDtypeStruct(s, d) for s, d in out_shapes],
        in_specs=specs,
        out_specs=[pl.BlockSpec(memory_space=pltpu.VMEM)] * len(out_shapes),
        scratch_shapes=list(scratch),
        compiler_params=pltpu.CompilerParams(vmem_limit_bytes=limit << 20),
    )(*args, *after)


PARTS = pltpu.VMEM((2, NI, RHS), BF16)
HALVES = [pltpu.VMEM((NI, RHS), BF16)] * 2
BLK = 256
FULL = ((NI, RHS), F32)
EDGE = ((NB, RHS), F32)
BLOCK = ((MODES, RHS), F32)
TOKEN = ((8, 128), F32)
FACES = [((FACE, RHS), F32)] * 2
BUNDLES = [((BUNDLE, RHS), F32)] * 2
PACKETS = BUNDLES + FACES


def put_packets(v, side0, side1, face0, face1):
    side0[...] = v[:BUNDLE]
    side1[...] = v[BUNDLE:SIDE]
    face0[...] = v[SIDE : SIDE + FACE]
    face1[...] = v[SIDE + FACE : SIDE + 2 * FACE]


def received(arrivals):
    side0, side1, face0, face1, corner0, corner1 = (ref[...] for ref in arrivals)
    end = CORNER + FACE
    return jnp.concatenate(
        [
            corner0[:CORNER],
            side0[CORNER:end],
            corner1[:CORNER],
            corner0[CORNER:],
            side1[CORNER:end],
            corner1[CORNER:],
            face0,
            face1,
            jnp.zeros((NB - SIDE - 2 * FACE, RHS), F32),
        ],
        axis=0,
    )


def turn_body(side0, side1, corner0, corner1):
    end = CORNER + FACE
    corner0[...] = jnp.concatenate([side0[:CORNER], side1[:CORNER]], axis=0)
    corner1[...] = jnp.concatenate([side0[end:], side1[end:]], axis=0)


def as_columns(row, width):
    return jnp.transpose(jnp.broadcast_to(row, (128, width)))


def slot_keys(lists, counts):
    turn_row, turn_col = lax.rem(lax.axis_index("row"), 2), lax.rem(lax.axis_index("col"), 2)
    blocks = []
    for p, q, size in SLOT_LISTS:
        a = p if p == 1 else p + 2 * (1 - p) * turn_row
        b = q if q == 1 else q + 2 * (1 - q) * turn_col
        ids = lax.broadcasted_iota(jnp.int32, (1, FACE), 1)
        row = jnp.where(ids < counts[a, b], lists[a, pl.ds(b, 1), :], -1).astype(F32)
        blocks.append(as_columns(row, FACE)[:size])
    return jnp.concatenate(blocks, axis=0)


SLOT_LISTS = (
    (2, 2, CORNER),
    (1, 2, FACE),
    (0, 2, CORNER),
    (2, 0, CORNER),
    (1, 0, FACE),
    (0, 0, CORNER),
    (2, 1, FACE),
    (0, 1, FACE),
)


def start_body(counts, lists, load, pick_out, *packets):
    keys = slot_keys(lists, counts)[:, 0:1]
    lanes = lax.broadcasted_iota(jnp.int32, (SLOTS, NI), 1).astype(F32)
    pick = jnp.where(keys == lanes, 1.0, 0.0).astype(BF16)
    pick_out[:SLOTS, :] = pick
    pick_out[SLOTS:, :] = jnp.zeros((NB - SLOTS, NI), BF16)
    put_packets(select(pick, split(load[...])), *packets)


def start_rest_body(pick, mult, load, modes, tile, place_out, weight_out, modes_out, edge_modes_out, tile_out, pre_out):
    def turned(cols):
        place_out[cols, :] = jnp.transpose(pick[:, cols].astype(F32)).astype(BF16)

    for blk in range(4):
        turned(slice(256 * blk, 256 * (blk + 1)))
    weight = 1.0 / mult[...].astype(F32)
    weight_out[...] = as_columns(weight, NI)
    high, low = split(modes[...] * weight)
    modes_out[0] = high
    modes_out[1] = low
    edge_modes_out[0] = dot(high, place_out[...]).astype(BF16)
    edge_modes_out[1] = dot(low, place_out[...]).astype(BF16)
    pre_out[...] = product(high, low, split(load[...]))
    a, b = split(jnp.transpose(tile[...]))
    tile_out[0] = a
    tile_out[1] = b


def matrix_body(scaled, *refs):
    mat, pick = refs[:2]
    full, edge, token = refs[-3:]
    token[...] = jnp.zeros_like(token)

    def halves(rows):
        value = mat[rows, :]
        if scaled:
            mult, column = refs[2:4]
            value = value * (1.0 / mult[...].astype(F32)) * column[rows, 0:1]
        a, b = split(value)
        full[0, rows, :] = a
        full[1, rows, :] = b

    by_rows(NI, 128, halves)

    def picked(i, carry):
        rows = pl.ds(pl.multiple_of(lax.rem(i, 2) * SIDE, SIDE), SIDE)
        edge[lax.div(i, 2), rows, :] = dot(pick[rows, :], full[lax.div(i, 2)]).astype(BF16)
        return carry

    lax.fori_loop(0, 4, picked, 0)


def corner_body(edge, place, out, token):
    token[...] = jnp.zeros_like(token)

    def level(i, carry):
        by_rows(NB, SIDE, lambda rows: step(i, rows))
        return carry

    def step(i, rows):
        out[i, rows, :] = dot(edge[i, rows, :], place[...]).astype(BF16)

    lax.fori_loop(0, 2, level, 0)


def close_body(sign, *refs):
    pre, edge_modes, edge_out, rhs_out = refs[-4:]
    edge = received(refs[:-4])
    edge_out[...] = edge
    t = product(edge_modes[0], edge_modes[1], split(edge))
    rhs = pre[...] + t if sign > 0 else pre[...] - t
    for i in range(rhs_out.shape[0]):
        rhs_out[i] = rhs


def rest_body(sign, base, edge, place, r_out, token):
    token[...] = jnp.zeros_like(token)
    parts = split(edge[...])

    def step(rows):
        arrived = select(place[rows, :], parts)
        r_out[rows, :] = base[rows, :] + arrived if sign > 0 else base[rows, :] - arrived

    by_rows(NI, BLK, step)


def final_body(*refs):
    mid, place, r_out = refs[-3:]
    parts = split(received(refs[:-3]))

    def step(rows):
        r_out[rows, :] = mid[rows, :] - select(place[rows, :], parts)

    by_rows(NI, 2 * BLK, step)


def coarse_body(shares, tile, out):
    gathered = jnp.concatenate([shares[i] for i in range(shares.shape[0])], axis=0)
    parts = split(gathered)

    def step(rows):
        out[rows, :] = product(tile[0, rows, :], tile[1, rows, :], parts)

    by_rows(tile.shape[1], 256, step)


def spread_body(shares, edge_modes, sol_out, *packets):
    sol = jnp.sum(shares[...], axis=0)
    sol_out[...] = sol
    put_packets(product(edge_modes[0], edge_modes[1], split(sol), dot_t), *packets)


def spread_rest_body(sol, modes, c_out, token):
    token[...] = jnp.zeros_like(token)
    parts = split(sol[...])

    def step(rows):
        c_out[rows, :] = product(modes[0, :, rows], modes[1, :, rows], parts, dot_t)

    by_rows(NI, BLK, step)


def apply_body(sign, *refs):
    pre, corner, edge_out = refs[-7:-4]
    edge = received(refs[:-7])
    edge_out[...] = edge
    rows = SIDE + 2 * FACE
    t = product(corner[0, :rows, :], corner[1, :rows, :], split(edge))
    put_packets(pre[:rows, :] + t if sign > 0 else pre[:rows, :] - t, *refs[-4:])


def apply_rest_body(fresh, *refs):
    edge, local, r, place, full = refs[:5]
    mid_out, x_out, token, high, low = refs[-5:]
    token[...] = jnp.zeros_like(token)
    parts = split(edge[...])

    def vector(rows):
        v = local[rows, :] + select(place[rows, :], parts)
        x_out[rows, :] = v if fresh else refs[5][rows, :] + v
        high[rows, :], low[rows, :] = split(v)

    by_rows(NI, BLK, vector)

    def applied(rows):
        mid_out[rows, :] = r[rows, :] - product(full[0, rows, :], full[1, rows, :], (high[...], low[...]))

    by_rows(NI, BLK, applied)


def solve_rest_body(edge, mid, place, full, r_out, g_out, token, high, low):
    token[...] = jnp.zeros_like(token)
    parts = split(edge[...])

    def vector(rows):
        r = mid[rows, :] - select(place[rows, :], parts)
        r_out[rows, :] = r
        high[rows, :], low[rows, :] = split(r)

    by_rows(NI, BLK, vector)

    def applied(rows):
        g_out[rows, :] = product(full[0, rows, :], full[1, rows, :], (high[...], low[...]))

    by_rows(NI, BLK, applied)


def local_body(mat, v, out, parts):
    keep_halves(parts, v)
    count = mat.shape[1]

    def step(rows):
        out[rows, :] = product(mat[0, rows, :], mat[1, rows, :], (parts[0], parts[1]))

    by_rows(count, min(count, SIDE), step)


def on_device(rows, cols, local_load, schur, solver, modes, inverse, share_rows, share_count, mult):
    both = ("row", "col")

    def shifted(value, target):
        pairs = [(a * cols + b, target(a, b)) for a in range(rows) for b in range(cols)]
        return lax.ppermute(value, both, pairs)

    def partner_of(i, k):
        return ((i + k) ^ 1) - k

    def by_col(value, k):
        def target(a, b):
            other = partner_of(b, k)
            return a * cols + other if 0 <= other < cols else (a ^ 1) * cols + b

        return shifted(value, target)

    def by_row(value, k):
        def target(a, b):
            other = partner_of(a, k)
            return other * cols + b if 0 <= other < rows else a * cols + (b ^ 4)

        return shifted(value, target)

    def depart(side0, side1, face0, face1):
        return by_col(side0, 0), by_col(side1, 1), by_row(face0, 0), by_row(face1, 1)

    def turn(arrived, *tokens):
        corners = call(turn_body, [((2 * CORNER, RHS), F32)] * 2, arrived[:2], after=tokens)
        return *arrived, by_row(corners[0], 0), by_row(corners[1], 1)

    def local(mat, v):
        return call(local_body, [((mat.shape[1], RHS), F32)], (mat, v), scratch=[PARTS])[0]

    lists, counts = share_rows[0, 0], share_count[0, 0]
    load = local_load[0, 0]

    pick, *packets = call(start_body, [((NB, NI), BF16), *PACKETS], (counts, lists, load), smem=1)
    arrived = depart(*packets)
    place, weight, modes_s, edge_modes, tile, pre = call(
        start_rest_body,
        [
            ((NI, NB), BF16),
            ((NI, 128), F32),
            ((2, MODES, NI), BF16),
            ((2, MODES, NB), BF16),
            ((2, 512, 256), BF16),
            BLOCK,
        ],
        (pick, mult[0], load, modes[0, 0], inverse[0, 0].reshape(256, 512)),
    )

    matrices = [((2, NI, NI), BF16), ((2, NB, NI), BF16), TOKEN]
    corner_shape = [((2, NB, NB), BF16), TOKEN]
    schur_full, schur_edge, schur_token = call(
        functools.partial(matrix_body, False), matrices, (schur[0, 0], pick)
    )
    schur_corner, corner_token = call(corner_body, corner_shape, (schur_edge, place))

    arrived = turn(arrived, schur_token)

    copies = ((rows, MODES, RHS), F32)
    edge, rhs = call(
        functools.partial(close_body, 1), [EDGE, copies], (*arrived, pre, edge_modes), after=(corner_token,)
    )
    x = mid = None
    for step in range(STEPS):
        shares = lax.all_to_all(rhs, "row", 0, 0, tiled=True)
        (partial,) = call(
            coarse_body,
            [((cols * MODES, RHS), F32)],
            (shares, tile),
        )
        shares = lax.all_to_all(partial.reshape(cols, MODES, RHS), "col", 0, 0, tiled=True)
        sol, *packets = call(spread_body, [BLOCK, *PACKETS], (shares, edge_modes))
        arrived = depart(*packets)
        c, token = call(spread_rest_body, [FULL, TOKEN], (sol, modes_s))
        sign, base = (1, load) if step == 0 else (-1, mid)
        r, r_token = call(
            functools.partial(rest_body, sign),
            [FULL, TOKEN],
            (base, edge, place),
            after=(token,),
        )
        if step == 0:
            solver_full, solver_edge, solver_token = call(
                functools.partial(matrix_body, True),
                matrices,
                (solver[0, 0], pick, mult[0], weight),
                after=(sol,),
            )
            solver_corner, corner_token = call(corner_body, corner_shape, (solver_edge, place))
            arrived = turn(arrived, r_token, solver_token)
        else:
            arrived = turn(arrived, r_token)
        pre = local(schur_edge, c)

        def apply(arrived, pre, v, r, x):
            edge, *packets = call(
                functools.partial(apply_body, 1), [EDGE, *PACKETS], (*arrived, pre, schur_corner)
            )
            arrived = depart(*packets)
            fresh = x is None
            args = [edge, v, r, place, schur_full] + ([] if fresh else [x])
            mid, x, token = call(functools.partial(apply_rest_body, fresh), [FULL, FULL, TOKEN], args, scratch=HALVES)
            return turn(arrived, token), mid, x

        arrived, mid, x = apply(arrived, pre, c, r, x)
        pre = local(solver_edge, mid)

        edge, *packets = call(functools.partial(apply_body, -1), [EDGE, *PACKETS], (*arrived, pre, solver_corner))
        arrived = depart(*packets)
        r, g, token = call(
            solve_rest_body, [FULL, FULL, TOKEN], (edge, mid, place, solver_full), scratch=HALVES
        )
        arrived = turn(arrived, token)
        pre = local(schur_edge, g)

        last = step == STEPS - 1
        arrived, mid, x = apply(arrived, pre, g, r, x)
        if last:
            (residual,) = call(final_body, [FULL], (*arrived, mid, place))
        else:
            pre = local(modes_s, mid)
            edge, rhs = call(functools.partial(close_body, -1), [EDGE, copies], (*arrived, pre, edge_modes))
    return x[None, None], residual[None, None]


def solution(mesh):
    grid = P("row", "col")
    rows, cols = mesh.shape["row"], mesh.shape["col"]
    return jax.shard_map(
        functools.partial(on_device, rows, cols),
        mesh=mesh,
        in_specs=(grid,) * 8,
        out_specs=(grid, grid),
        check_vma=False,
    )
```
